128 devices in a mesh: outer: 4 (over z_lo, core), inner: 32 (over z_hi, y, x).
Axes of the slice: x: 4, y: 4, z: 4 (z_hi: 2, z_lo: 2; z = z_hi * 2 + z_lo), core: 2. Of those that a mesh axis runs over, the one named last changes fastest.
Arguments:
- inputs: bfloat16 [131072, 1024], P(('outer', 'inner')), may hold values from -24 to 24
- queries: bfloat16 [131072, 1024], P(('outer', 'inner')), may hold values from -6 to 6
- keys: bfloat16 [131072, 1024], P(('outer', 'inner')), may hold values from -6 to 6
- values: bfloat16 [131072, 1024], P(('outer', 'inner')), may hold values from -6 to 6
- out_grad: bfloat16 [131072, 1024], P(('outer', 'inner')), may hold values from -6 to 6
- master: float32 [1024, 1024], P('inner'), may hold values from -0.1875 to 0.1875
- moment1: float32 [1024, 1024], P('inner'), may hold values from -6 to 6
- moment2: float32 [1024, 1024], P('inner'), may hold values from 0.05 to 2
Outputs:
- query_grad: bfloat16 [131072, 1024], P(('outer', 'inner'))
- key_grad: bfloat16 [131072, 1024], P(('outer', 'inner'))
- new_master: float32 [1024, 1024], P('inner')
- new_moment1: float32 [1024, 1024], P('inner')
- new_moment2: float32 [1024, 1024], P('inner')
- weights: bfloat16 [1024, 1024], replicated
The draws below stay inside these ranges and needn't reach their ends.
All inputs are finite; a program needn't handle non-finite values.
Results may differ from the reference program's by a relative error of at most 0.008.
Values may be sent and summed in bfloat16 or wider, within the bound.
A program may use at most 192 MiB of HBM per device.

```python
import math
import jax
import jax.numpy as jnp
from jax import lax

D = 1024
H = 8
HD = 128
BLK = 512
TOKENS = 131072


def raised(entries, stream_key, source, target, shards_of, factor):
    owner, partner = [(jnp.arange(entries.shape[dim]) // (entries.shape[dim] // shards_of)).reshape([-1 if axis == dim else 1 for axis in range(entries.ndim)]) for dim in (source, target)]
    chosen = jax.random.permutation(stream_key, shards_of)[partner]
    strong = (owner == chosen) | (owner == (partner + shards_of // 2) % shards_of)
    return jnp.where(strong, factor * entries, entries)


def block_levels(own_key, dims, pieces, low, largest):
    def one(axis_at, blocks):
        heights = jax.random.uniform(jax.random.fold_in(jax.random.fold_in(own_key, 6), axis_at), (blocks,), jnp.float32, low / len(pieces), largest / len(pieces))
        return jnp.repeat(jnp.exp(heights), dims[axis_at] // blocks).reshape((-1,) + (1,) * (len(dims) - axis_at - 1))

    factor_of = one(*pieces[0])
    for cut in pieces[1:]:
        factor_of = factor_of * one(*cut)
    return factor_of


def noise(stream_key, dims, width, limit, split=(), held_as=jnp.bfloat16):
    drawn = jax.random.normal(stream_key, dims, jnp.float32) * width
    if len(split) > 0:
        drawn = block_levels(stream_key, dims, split, -0.22, 0.18) * drawn
    return jnp.clip(drawn, min=-limit, max=limit).astype(held_as)


def bell_draw_with(rng, dims, spread, reach, pieces, heavy, kind=jnp.bfloat16):
    drawn = spread * jax.random.normal(rng, dims, jnp.float32)
    if pieces:
        drawn = drawn * block_levels(rng, dims, pieces, -0.22, 0.18)
    return jnp.clip(raised(drawn, jax.random.fold_in(rng, 3), *heavy), -reach, reach).astype(kind)


def setup_inputs(seed: int = 0) -> dict:
    arg_keys = jax.random.split(jax.random.key(seed), 9)
    inputs = bell_draw_with(arg_keys[0], (TOKENS, D), 1.0, 24.0, ((0, 128),), (0, 1, 128, 5.5))
    queries = noise(arg_keys[1], (TOKENS, D), 1.0, 6.0, ((0, 128),))
    keys = noise(arg_keys[2], (TOKENS, D), 1.0, 6.0, ((0, 128),))
    values = noise(arg_keys[3], (TOKENS, D), 1.0, 6.0, ((0, 128),))
    out_grad = noise(arg_keys[4], (TOKENS, D), 1.0, 6.0, ((0, 128),))
    master = noise(arg_keys[5], (D, D), D ** -0.5, 0.1875, ((0, 32),), jnp.float32)
    moment1 = noise(arg_keys[6], (D, D), 1.0, 6.0, ((0, 32),), jnp.float32)
    moment2 = jnp.clip(jnp.exp(math.log(2.0) - 3.6888794 * jax.random.uniform(arg_keys[7], (D, D), jnp.float32) ** block_levels(arg_keys[7], (D, D), ((0, 32),), -0.2, 0.2)), 0.05, 2.0)
    return {"inputs": inputs, "queries": queries, "keys": keys, "values": values, "out_grad": out_grad, "master": master, "moment1": moment1, "moment2": moment2}


def reference(inputs, queries, keys, values, out_grad, master, moment1, moment2):
    blocks = TOKENS // BLK
    att_scale = 1.0 / math.sqrt(HD * TOKENS)
    grad_scale = 1.0 / math.sqrt(TOKENS)
    shape_four = (blocks, BLK, H, HD)
    query_blocks = queries.reshape(shape_four)
    key_blocks = keys.reshape(shape_four)
    value_blocks = values.reshape(shape_four)
    grad_blocks = out_grad.reshape(shape_four)
    highest_setting = lax.Precision.HIGHEST

    def block_states(items):
        query_b, key_block_rows, value_block_rows, block_gradient = [item.astype(jnp.float32) for item in items]
        key_value_state = jnp.einsum('yze,yza->zea', key_block_rows, value_block_rows, precision=highest_setting)
        grad_query = jnp.einsum('thv,thk->hvk', block_gradient, query_b, precision=highest_setting)
        return (key_value_state, grad_query)
    kv_block, qg_block = lax.map(block_states, (query_blocks, key_blocks, value_blocks, grad_blocks))
    zero_state = jnp.zeros((1, H, HD, HD), jnp.float32)
    key_value_prior = jnp.concatenate([zero_state, jnp.cumsum(kv_block, 0)[:-1]], 0)
    qg_reverse = jnp.cumsum(qg_block[::-1], 0)[::-1]
    qg_after = jnp.concatenate([qg_reverse[1:], zero_state], 0)
    causal = jnp.arange(BLK)[:, None] >= jnp.arange(BLK)[None, :]

    def block_grads(items):
        query_b, key_block_rows, value_block_rows, block_gradient, prior_block_state, after_b = items
        query_f = query_b.astype(jnp.float32)
        key_f = key_block_rows.astype(jnp.float32)
        value_f = value_block_rows.astype(jnp.float32)
        flat_gradient = block_gradient.astype(jnp.float32)
        scores = jnp.einsum('thv,shv->hts', flat_gradient, value_f, precision=highest_setting)
        scores = jnp.where(causal[None], scores, 0.0).astype(jnp.bfloat16).astype(jnp.float32)
        query_gradient = jnp.einsum('hts,shk->thk', scores, key_f, precision=highest_setting)
        query_gradient = query_gradient + jnp.einsum('rgn,gfn->rgf', flat_gradient, prior_block_state, precision=highest_setting)
        dkey = jnp.einsum('hts,thk->shk', scores, query_f, precision=highest_setting)
        dkey = dkey + jnp.einsum('shv,hvk->shk', value_f, after_b, precision=highest_setting)
        query_gradient = (query_gradient * att_scale).astype(jnp.bfloat16).reshape(BLK, D)
        dkey = (dkey * att_scale).astype(jnp.bfloat16).reshape(BLK, D)
        return (query_gradient, dkey)
    query_grad, key_grad = lax.map(block_grads, (query_blocks, key_blocks, value_blocks, grad_blocks, key_value_prior, qg_after))
    input_blocks = inputs.reshape(blocks, BLK, D)

    def accumulate(total, items):
        input_b, dkey_b = items
        term = jnp.dot(input_b.astype(jnp.float32).T, dkey_b.astype(jnp.float32), precision=highest_setting)
        return (total + term, None)
    grad, unused = lax.scan(accumulate, jnp.zeros((D, D), jnp.float32), (input_blocks, key_grad))
    grad = grad * grad_scale
    new_moment1 = 0.9 * moment1 + 0.1 * grad
    new_moment2 = 0.95 * moment2 + 0.05 * grad * grad
    new_master = master - 0.01 * (new_moment1 / (jnp.sqrt(new_moment2) + 1e-08) + 0.1 * master)
    return (query_grad.reshape(TOKENS, D), key_grad.reshape(TOKENS, D), new_master, new_moment1, new_moment2, new_master.astype(jnp.bfloat16))
```

```python
import math

import jax
import jax.numpy as jnp
from jax import lax
from jax.experimental import pallas as pl
from jax.experimental.pallas import tpu as pltpu
from jax.sharding import PartitionSpec as P

H = 8
HD = 128
BLK = 512
HALF = BLK // 2
PLANE = 16
GROUP = 8
MESH = pl.DeviceIdType.MESH
F32 = jnp.float32
BF16 = jnp.bfloat16
ANY = pl.BlockSpec(memory_space=pl.ANY)
VMEM = pl.BlockSpec(memory_space=pltpu.VMEM)


def nt(a, b):
    return lax.dot_general(a, b, (((1,), (1,)), ((), ())), preferred_element_type=F32)


def tn(a, b):
    return lax.dot_general(a, b, (((0,), (0,)), ((), ())), preferred_element_type=F32)


def nn(a, b):
    return lax.dot_general(a, b, (((1,), (0,)), ((), ())), preferred_element_type=F32)


def place():
    outer, inner = lax.axis_index("outer"), lax.axis_index("inner")
    return outer, inner, outer // 2, outer % 2, inner // PLANE, inner % PLANE


def greet(barrier, peers):
    for peer in peers:
        pl.semaphore_signal(barrier, inc=1, device_id=peer, device_id_type=MESH)


def send(src, dst, send_sem, recv_sem, peer):
    copy = pltpu.make_async_remote_copy(
        src_ref=src, dst_ref=dst, send_sem=send_sem, recv_sem=recv_sem, device_id=peer, device_id_type=MESH
    )
    copy.start()
    return copy


def arrived(ref, sem):
    pltpu.make_async_copy(ref, ref, sem).wait()


def scan_kernel(
    q_hbm, k_hbm, v_hbm, g_hbm,
    kvst_ref, qgst_ref, qi_hbm, ki_hbm,
    q, k, v, g, qi, ki, own, got, local, total, totals, back, final, kv0, qg1,
    in_sem, out_sem, s1, r1, s2, r2, s3, r3,
):
    outer, inner, z_lo, core, z_hi, p = place()
    at = z_lo * 4 + core * 2 + z_hi
    plane = [(outer, z_hi * PLANE + (p + o) % PLANE) for o in range(1, PLANE)]
    group = []
    for o in range(1, GROUP):
        other = (at + o) % GROUP
        group.append((other // 2, (other % 2) * PLANE + p))
    barrier = pltpu.get_barrier_semaphore()
    greet(barrier, plane + group)
    loads = []
    for n, (src, dst) in enumerate(((k_hbm, k), (v_hbm, v), (g_hbm, g), (q_hbm, q))):
        copy = pltpu.make_async_copy(src, dst, in_sem.at[n])
        copy.start()
        loads.append(copy)

    loads[0].wait()
    loads[1].wait()

    @pl.loop(0, H)
    def _(h):
        cols = pl.ds(pl.multiple_of(h * HD, HD), HD)
        first = tn(k[0:BLK, cols], v[0:BLK, cols])
        second = tn(k[BLK : 2 * BLK, cols], v[BLK : 2 * BLK, cols])
        kv0[h] = first
        both = (first + second).astype(BF16)
        own[2 * h, 0] = both[0 : HD // 2]
        own[2 * h + 1, 0] = both[HD // 2 :]

    loads[2].wait()
    loads[3].wait()

    @pl.loop(0, H)
    def _(h):
        cols = pl.ds(pl.multiple_of(h * HD, HD), HD)
        first = tn(g[0:BLK, cols], q[0:BLK, cols])
        second = tn(g[BLK : 2 * BLK, cols], q[BLK : 2 * BLK, cols])
        qg1[h] = second
        both = (first + second).astype(BF16)
        own[2 * h, 1] = both[0 : HD // 2]
        own[2 * h + 1, 1] = both[HD // 2 :]

    pl.semaphore_wait(barrier, PLANE - 1 + GROUP - 1)

    sent = []
    for o in range(1, PLANE):
        to = (p + o) % PLANE
        sent.append(send(own.at[to], got.at[p], s1.at[o], r1.at[p], plane[o - 1]))

    rows = lax.broadcasted_iota(jnp.int32, (HALF, HALF), 0)
    lanes = lax.broadcasted_iota(jnp.int32, (HALF, HALF), 1)
    causal = rows >= lanes

    def intra(step):
        top = pl.multiple_of((step // H) * BLK, BLK)
        cols = pl.ds(pl.multiple_of((step % H) * HD, HD), HD)
        a, b = pl.ds(top, HALF), pl.ds(pl.multiple_of(top + HALF, HALF), HALF)
        g0, g1, v0, v1 = g[a, cols], g[b, cols], v[a, cols], v[b, cols]
        s00 = jnp.where(causal, nt(g0, v0), 0.0).astype(BF16)
        s10 = nt(g1, v0).astype(BF16)
        s11 = jnp.where(causal, nt(g1, v1), 0.0).astype(BF16)
        k0, k1, q0, q1 = k[a, cols], k[b, cols], q[a, cols], q[b, cols]
        qi[a, cols] = nn(s00, k0).astype(BF16)
        qi[b, cols] = (nn(s10, k0) + nn(s11, k1)).astype(BF16)
        ki[a, cols] = (tn(s00, q0) + tn(s10, q1)).astype(BF16)
        ki[b, cols] = tn(s11, q1).astype(BF16)

    pl.loop(0, 8)(intra)

    got[p] = own[p]
    for o in range(1, PLANE):
        src = (p + PLANE - o) % PLANE
        arrived(got.at[src], r1.at[src])

    run = jnp.zeros((HD // 2, HD), F32)
    for j in range(PLANE):
        local[j, 0] = run
        run = run + got[j, 0].astype(F32)
    total[0] = run.astype(BF16)
    run = jnp.zeros((HD // 2, HD), F32)
    for j in reversed(range(PLANE)):
        local[j, 1] = run
        run = run + got[j, 1].astype(F32)
    total[1] = run.astype(BF16)

    for o in range(1, GROUP):
        sent.append(send(total, totals.at[at], s2.at[o], r2.at[at], group[o - 1]))

    pl.loop(8, 12)(intra)

    for o in range(1, GROUP):
        src = (at + GROUP - o) % GROUP
        arrived(totals.at[src], r2.at[src])
    totals[at] = total[...]
    before = jnp.zeros((HD // 2, HD), F32)
    after = jnp.zeros((HD // 2, HD), F32)
    for j in range(GROUP):
        before = before + jnp.where(j < at, totals[j, 0].astype(F32), 0.0)
        after = after + jnp.where(j > at, totals[j, 1].astype(F32), 0.0)
    for j in range(PLANE):
        back[j, 0] = (local[j, 0] + before).astype(BF16)
        back[j, 1] = (local[j, 1] + after).astype(BF16)
    for o in range(1, PLANE):
        to = (p + o) % PLANE
        sent.append(send(back.at[to], final.at[p], s3.at[o], r3.at[p], plane[o - 1]))

    pl.loop(12, 16)(intra)
    outs = []
    for n, (src, dst) in enumerate(((qi, qi_hbm), (ki, ki_hbm))):
        copy = pltpu.make_async_copy(src, dst, out_sem.at[n])
        copy.start()
        outs.append(copy)

    final[p] = back[p]
    for o in range(1, PLANE):
        src = (p + PLANE - o) % PLANE
        arrived(final.at[src], r3.at[src])

    for h in range(H):
        for part in range(2):
            piece, half = 2 * h + part, slice(part * HD // 2, (part + 1) * HD // 2)
            kv_in, qg_in = final[piece, 0], final[piece, 1]
            kvst_ref[0, h, half] = kv_in
            kvst_ref[1, h, half] = (kv_in.astype(F32) + kv0[h, half]).astype(BF16)
            qgst_ref[1, h, half] = qg_in
            qgst_ref[0, h, half] = (qg_in.astype(F32) + qg1[h, half]).astype(BF16)

    for copy in sent:
        copy.wait_send()
    for copy in outs:
        copy.wait()


def scan_call(q, k, v, g):
    piece = (2, HD // 2, HD)
    big = pltpu.VMEM(q.shape, BF16)
    state = jax.ShapeDtypeStruct((2, H, HD, HD), BF16)
    full = jax.ShapeDtypeStruct(q.shape, BF16)
    dma = pltpu.SemaphoreType.DMA
    return pl.pallas_call(
        scan_kernel,
        out_shape=(state, state, full, full),
        in_specs=[ANY] * 4,
        out_specs=(VMEM, VMEM, ANY, ANY),
        scratch_shapes=[
            big, big, big, big, big, big,
            pltpu.VMEM((PLANE,) + piece, BF16),
            pltpu.VMEM((PLANE,) + piece, BF16),
            pltpu.VMEM((PLANE,) + piece, F32),
            pltpu.VMEM(piece, BF16),
            pltpu.VMEM((GROUP,) + piece, BF16),
            pltpu.VMEM((PLANE,) + piece, BF16),
            pltpu.VMEM((PLANE,) + piece, BF16),
            pltpu.VMEM((H, HD, HD), F32),
            pltpu.VMEM((H, HD, HD), F32),
            dma((4,)), dma((2,)),
            dma((PLANE,)), dma((PLANE,)), dma((GROUP,)), dma((GROUP,)), dma((PLANE,)), dma((PLANE,)),
        ],
        compiler_params=pltpu.CompilerParams(collective_id=0, has_side_effects=True, vmem_limit_bytes=48 << 20),
        name="scan",
    )(q, k, v, g)


def grads_kernel(scale, kvst, qgst, g, v, qi, ki, dq, dk):
    for h in range(H):
        cols = slice(h * HD, (h + 1) * HD)
        dq[:, cols] = ((qi[:, cols].astype(F32) + nt(g[:, cols], kvst[0, h])) * scale).astype(BF16)
        dk[:, cols] = ((ki[:, cols].astype(F32) + nn(v[:, cols], qgst[0, h])) * scale).astype(BF16)


def grads_call(scale, kvst, qgst, g, v, qi, ki):
    rows, width = g.shape
    tile = 256
    per = BLK // tile
    state = pl.BlockSpec((1, H, HD, HD), lambda i: (i // per, 0, 0, 0))
    band = pl.BlockSpec((tile, width), lambda i: (i, 0))
    full = jax.ShapeDtypeStruct((rows, width), BF16)
    return pl.pallas_call(
        lambda *refs: grads_kernel(scale, *refs),
        out_shape=(full, full),
        grid=(rows // tile,),
        in_specs=[state, state, band, band, band, band],
        out_specs=(band, band),
        compiler_params=pltpu.CompilerParams(vmem_limit_bytes=32 << 20),
        name="grads",
    )(kvst, qgst, g, v, qi, ki)


def update_kernel(
    grad_scale, x_hbm, dk_hbm, master, m1, m2,
    new_master, new_m1, new_m2, w_hbm,
    xs, dk, give, mine, r0, r1, b, r2, c, r3, w, wide, far,
    in_sem, out_sem, s0, q0, s1, q1, s2, q2, s3, q3, s4, q4, s5, q5, s6, q6,
):
    outer, inner, z_lo, core, z_hi, p = place()
    y, x = p // 4, p % 4
    z = z_hi * 2 + z_lo
    partner = (z_lo * 2 + 1 - core, inner)
    along_x = [(outer, z_hi * PLANE + y * 4 + (x + o) % 4) for o in range(1, 4)]
    along_y = [(outer, z_hi * PLANE + ((y + o) % 4) * 4 + x) for o in range(1, 4)]
    seat = core * 4 + z
    group, group_hi = [], []
    for o in range(1, GROUP):
        other = (seat + o) % GROUP
        other_core, other_z = other // 4, other % 4
        group.append(((other_z % 2) * 2 + other_core, (other_z // 2) * PLANE + p))
        group_hi.append(other_z // 2)
    beside = (z + 4 + 2 * z_lo - 1) % 4
    beside_outer, beside_inner = (beside % 2) * 2 + core, (beside // 2) * PLANE
    near_x = [(beside_outer, beside_inner + y * 4 + (x + o) % 4) for o in range(4)]
    near_y = [(beside_outer, beside_inner + ((y + o) % 4) * 4 + x) for o in range(4)]
    peers = along_x + along_y + group + near_x[1:] + near_y[1:]
    barrier = pltpu.get_barrier_semaphore()
    greet(barrier, peers)
    loads = []
    for n, (src, dst) in enumerate(((x_hbm, xs), (dk_hbm, dk))):
        copy = pltpu.make_async_copy(src, dst, in_sem.at[n])
        copy.start()
        loads.append(copy)
    for copy in loads:
        copy.wait()

    def product(half, color, keep):
        cols = pl.ds(pl.multiple_of(half * 512 + color * 256, 256), 256)

        @pl.loop(0, 4)
        def _(m):
            got = tn(xs[:, pl.ds(pl.multiple_of(m * 256, 256), 256)], dk[:, cols]) * grad_scale
            hi = m // 2
            for part in range(8):
                row, at_x = (m % 2) * 2 + part // 4, part % 4
                for lo in range(2):
                    piece = got[part * 32 : part * 32 + 32, lo * 128 : lo * 128 + 128]
                    if color == 0:
                        keep[color, at_x, row, hi, lo] = piece.astype(keep.dtype)
                    else:
                        keep[color, row, at_x, hi, lo] = piece.astype(keep.dtype)

    sent = []
    product(1 - core, 0, give)
    pl.semaphore_wait(barrier, len(peers))
    sent.append(send(give.at[0], r0.at[0], s0.at[0], q0.at[0], partner))
    product(1 - core, 1, give)
    sent.append(send(give.at[1], r0.at[1], s0.at[1], q0.at[1], partner))
    product(core, 0, mine)
    product(core, 1, mine)

    lines = ((x, along_x), (y, along_y))
    for color in range(2):
        here, line = lines[color]
        arrived(r0.at[color], q0.at[color])
        for o in (2, 1, 3):
            to = (here + o) % 4
            b[color, o] = (mine[color, to] + r0[color, to].astype(F32)).astype(BF16)
            sent.append(send(b.at[color, o], r1.at[color, o], s1.at[color, o], q1.at[color, o], line[o - 1]))
        mine[color, here] = mine[color, here] + r0[color, here].astype(F32)
    for color in range(2):
        here = lines[color][0]
        there, line = lines[1 - color]
        for o in range(1, 4):
            arrived(r1.at[color, o], q1.at[color, o])
        mine[color, here] = (
            mine[color, here] + r1[color, 1].astype(F32) + r1[color, 2].astype(F32) + r1[color, 3].astype(F32)
        )
        for o in (2, 1, 3):
            to = (there + o) % 4
            c[color, o] = mine[color, here, to].astype(BF16)
            sent.append(send(c.at[color, o], r2.at[color, o], s2.at[color, o], q2.at[color, o], line[o - 1]))
    for color in range(2):
        here, there = lines[color][0], lines[1 - color][0]
        for o in range(1, 4):
            arrived(r2.at[color, o], q2.at[color, o])
        done = (
            mine[color, here, there] + r2[color, 1].astype(F32) + r2[color, 2].astype(F32) + r2[color, 3].astype(F32)
        ).astype(BF16)
        w[0, color] = done[0]
        w[1, color] = done[1]
    for o in range(1, GROUP):
        sent.append(send(w.at[group_hi[o - 1]], r3.at[seat], s3.at[o], q3.at[seat], group[o - 1]))
    r3[seat] = w[z_hi]
    for o in range(1, GROUP):
        src = (seat + GROUP - o) % GROUP
        arrived(r3.at[src], q3.at[src])

    for t in range(8):
        half, color, lo = t // 4, (t // 2) % 2, t % 2
        cols = slice(t * 128, t * 128 + 128)
        grad = r3[half * 4, color, lo].astype(F32)
        for n in range(1, 4):
            grad = grad + r3[half * 4 + n, color, lo].astype(F32)
        first = 0.9 * m1[:, cols] + 0.1 * grad
        second = 0.95 * m2[:, cols] + 0.05 * grad * grad
        old = master[:, cols]
        new = old - 0.01 * (first / (jnp.sqrt(second) + 1e-08) + 0.1 * old)
        new_m1[:, cols] = first
        new_m2[:, cols] = second
        new_master[:, cols] = new

    for color in range(2):
        here, there = lines[color][0], lines[1 - color][0]
        cols = pl.ds(pl.multiple_of(core * 512 + color * 256, 256), 256)
        wide[color, here, z_hi, there] = new_master[:, cols].astype(BF16)
    for color in range(2):
        here, there = lines[color][0], lines[1 - color][0]
        line = lines[1 - color][1]
        near = near_y if color == 0 else near_x
        spot = wide.at[color, here, z_hi, there]
        for o in (2, 1, 3, 0):
            if o:
                sent.append(send(spot, spot, s4.at[color, 0, o], q4.at[color, 0, o], line[o - 1]))
            sent.append(send(spot, spot, s4.at[color, 1, o], q4.at[color, 1, o], near[o]))
    for color in range(2):
        here, there = lines[color][0], lines[1 - color][0]
        line = lines[color][1]
        for o in range(4):
            src = (there + 4 - o) % 4
            if o:
                arrived(wide.at[color, here, z_hi, src], q4.at[color, 0, o])
            arrived(wide.at[color, here, 1 - z_hi, src], q4.at[color, 1, o])
        spot = wide.at[color, here]
        for o in (2, 1, 3):
            sent.append(send(spot, spot, s5.at[color, o], q5.at[color, o], line[o - 1]))
        sent.append(send(spot, far.at[color, here], s6.at[color, 0], q6.at[color, 0], partner))

    outs = []

    def put(src, half, color, at, n):
        cols = pl.ds(pl.multiple_of(half * 512 + color * 256, 256), 256)
        dst = w_hbm.at[:, :, at, :, cols] if color == 0 else w_hbm.at[:, at, :, :, cols]
        copy = pltpu.make_async_copy(src, dst, out_sem.at[n])
        copy.start()
        outs.append(copy)

    for color in range(2):
        here = lines[color][0]
        put(wide.at[color, here], core, color, here, color * 8)
    for o in (1, 3, 2):
        for color in range(2):
            here = lines[color][0]
            src = (here + 4 - o) % 4
            arrived(wide.at[color, src], q5.at[color, o])
            sent.append(send(wide.at[color, src], far.at[color, src], s6.at[color, o], q6.at[color, o], partner))
            put(wide.at[color, src], core, color, src, color * 8 + o)
    for o in (0, 1, 3, 2):
        for color in range(2):
            here = lines[color][0]
            src = (here + 4 - o) % 4
            arrived(far.at[color, src], q6.at[color, o])
            put(far.at[color, src], 1 - core, color, src, color * 8 + 4 + o)
    for copy in sent:
        copy.wait_send()
    for copy in outs:
        copy.wait()


def update_call(grad_scale, inputs, dk, master, m1, m2):
    rows, width = master.shape
    shard = jax.ShapeDtypeStruct(master.shape, F32)
    dma = pltpu.SemaphoreType.DMA
    tile = (32, 128)
    wide = (2, 4, 2, 4, 32, 256)
    return pl.pallas_call(
        lambda *refs: update_kernel(grad_scale, *refs),
        out_shape=(shard, shard, shard, jax.ShapeDtypeStruct((2, 4, 4, 32, width), BF16)),
        in_specs=[ANY, ANY, VMEM, VMEM, VMEM],
        out_specs=(VMEM, VMEM, VMEM, ANY),
        scratch_shapes=[
            pltpu.VMEM(inputs.shape, BF16),
            pltpu.VMEM(dk.shape, BF16),
            pltpu.VMEM((2, 4, 4, 2, 2) + tile, BF16),
            pltpu.VMEM((2, 4, 4, 2, 2) + tile, F32),
            pltpu.VMEM((2, 4, 4, 2, 2) + tile, BF16),
            pltpu.VMEM((2, 4, 4, 2, 2) + tile, BF16),
            pltpu.VMEM((2, 4, 4, 2, 2) + tile, BF16),
            pltpu.VMEM((2, 4, 2, 2) + tile, BF16),
            pltpu.VMEM((2, 4, 2, 2) + tile, BF16),
            pltpu.VMEM((GROUP, 2, 2) + tile, BF16),
            pltpu.VMEM((2, 2, 2) + tile, BF16),
            pltpu.VMEM(wide, BF16),
            pltpu.VMEM(wide, BF16),
            dma((2,)), dma((16,)),
            dma((2,)), dma((2,)), dma((2, 4)), dma((2, 4)), dma((2, 4)), dma((2, 4)),
            dma((GROUP,)), dma((GROUP,)), dma((2, 2, 4)), dma((2, 2, 4)),
            dma((2, 4)), dma((2, 4)), dma((2, 4)), dma((2, 4)),
        ],
        compiler_params=pltpu.CompilerParams(collective_id=1, has_side_effects=True, vmem_limit_bytes=48 << 20),
        name="update",
    )(inputs, dk, master, m1, m2)


def local(inputs, queries, keys, values, out_grad, master, moment1, moment2):
    total_tokens = inputs.shape[0] * lax.axis_size("outer") * lax.axis_size("inner")
    att_scale = 1.0 / math.sqrt(HD * total_tokens)
    grad_scale = 1.0 / math.sqrt(total_tokens)
    kvst, qgst, qi, ki = scan_call(queries, keys, values, out_grad)
    query_grad, key_grad = grads_call(att_scale, kvst, qgst, out_grad, values, qi, ki)
    new_master, new_m1, new_m2, weights = update_call(grad_scale, inputs, key_grad, master, moment1, moment2)
    return query_grad, key_grad, new_master, new_m1, new_m2, weights.reshape(inputs.shape[1], -1)


def solution(mesh):
    tokens, shard = P(("outer", "inner"), None), P("inner", None)
    return jax.shard_map(
        local,
        mesh=mesh,
        in_specs=(tokens,) * 5 + (shard,) * 3,
        out_specs=(tokens, tokens, shard, shard, shard, P()),
        check_vma=False,
    )
```

```python
import math

import jax
import jax.numpy as jnp
from jax import lax
from jax.experimental import pallas as pl
from jax.experimental.pallas import tpu as pltpu
from jax.sharding import PartitionSpec as P

H = 8
HD = 128
BLK = 512
HALF = BLK // 2
PLANE = 16
N1, N2, K1, M1, M2 = 6, 10, 4, 4, 10
GROUP = 8
MESH = pl.DeviceIdType.MESH
F32 = jnp.float32
BF16 = jnp.bfloat16
ANY = pl.BlockSpec(memory_space=pl.ANY)
VMEM = pl.BlockSpec(memory_space=pltpu.VMEM)


def nt(a, b):
    return lax.dot_general(a, b, (((1,), (1,)), ((), ())), preferred_element_type=F32)


def tn(a, b):
    return lax.dot_general(a, b, (((0,), (0,)), ((), ())), preferred_element_type=F32)


def nn(a, b):
    return lax.dot_general(a, b, (((1,), (0,)), ((), ())), preferred_element_type=F32)


def place():
    outer, inner = lax.axis_index("outer"), lax.axis_index("inner")
    return outer, inner, outer // 2, outer % 2, inner // PLANE, inner % PLANE


def greet(barrier, peers):
    for peer in peers:
        pl.semaphore_signal(barrier, inc=1, device_id=peer, device_id_type=MESH)


def send(src, dst, send_sem, recv_sem, peer):
    copy = pltpu.make_async_remote_copy(
        src_ref=src, dst_ref=dst, send_sem=send_sem, recv_sem=recv_sem, device_id=peer, device_id_type=MESH
    )
    copy.start()
    return copy


def arrived(ref, sem):
    pltpu.make_async_copy(ref, ref, sem).wait()


def adam(grad, master, m1, m2):
    first = 0.9 * m1 + 0.1 * grad
    second = 0.95 * m2 + 0.05 * grad * grad
    new = master - 0.01 * (first / (jnp.sqrt(second) + 1e-08) + 0.1 * master)
    return new, first, second


def diagonal(first, second):
    zero = jnp.zeros_like(first)
    return jnp.concatenate([jnp.concatenate([first, zero], 1), jnp.concatenate([zero, second], 1)], 0)


def kernel(
    att_scale, grad_scale,
    x_hbm, q_hbm, k_hbm, v_hbm, g_hbm, master, m1, m2,
    dq_hbm, dk_hbm, w_hbm, grad_ref,
    x, q, k, v, g, xt, ki, xv, dq, dk, pre, scores, qg1, kv0,
    own, got, local, total, totals, back, final,
    give, mine, r0, r1, b, r2, c, r3, w, done, summed, other_sum, wide, far,
    in_sem, out_sem, a1, e1, a2, e2, a3, e3,
    s0, q0, s1, q1, s2, q2, s3, q3, s4, q4, s5, q5, s6, q6, pair_sem,
):
    outer, inner, z_lo, core, z_hi, p = place()
    at_y, at_x = p // 4, p % 4
    z = z_hi * 2 + z_lo
    at = z_lo * 4 + core * 2 + z_hi
    plane = [(outer, z_hi * PLANE + (p + o) % PLANE) for o in range(1, PLANE)]
    ranked = []
    for o in range(1, GROUP):
        other = (at + o) % GROUP
        ranked.append((other // 2, (other % 2) * PLANE + p))
    partner = (z_lo * 2 + 1 - core, inner)
    along_x = [(outer, z_hi * PLANE + at_y * 4 + (at_x + o) % 4) for o in range(1, 4)]
    along_y = [(outer, z_hi * PLANE + ((at_y + o) % 4) * 4 + at_x) for o in range(1, 4)]
    beside = (z + 4 + 2 * z_lo - 1) % 4
    beside_outer, beside_inner = (beside % 2) * 2 + core, (beside // 2) * PLANE
    near_x = [(beside_outer, beside_inner + at_y * 4 + (at_x + o) % 4) for o in range(4)]
    near_y = [(beside_outer, beside_inner + ((at_y + o) % 4) * 4 + at_x) for o in range(4)]
    peers = plane + ranked + near_x[1:] + near_y[1:]
    barrier = pltpu.get_barrier_semaphore()
    greet(barrier, peers)
    loads = []
    for n, (src, dst) in enumerate(((g_hbm, g), (q_hbm, q), (k_hbm, k), (v_hbm, v), (x_hbm, x))):
        copy = pltpu.make_async_copy(src, dst, in_sem.at[n])
        copy.start()
        loads.append(copy)
    sent = []
    QG, KV = 0, 1

    def head_cols(h):
        return pl.ds(pl.multiple_of(h * HD, HD), HD)

    def states(stream, left, right, keep, kept):
        @pl.loop(0, H)
        def _(h):
            cols = head_cols(h)
            blocks = [tn(left[n * BLK : (n + 1) * BLK, cols], right[n * BLK : (n + 1) * BLK, cols]) for n in range(2)]
            keep[h] = blocks[kept].astype(keep.dtype)
            both = (blocks[0] + blocks[1]).astype(BF16)
            own[stream, 2 * h] = both[0 : HD // 2]
            own[stream, 2 * h + 1] = both[HD // 2 :]

    def spread(stream):
        for o in range(1, PLANE):
            to = (p + o) % PLANE
            sent.append(send(own.at[stream, to], got.at[stream, p], a1.at[stream, o], e1.at[stream, p], plane[o - 1]))
        got[stream, p] = own[stream, p]

    def gather(stream):
        for o in range(1, PLANE):
            src = (p + PLANE - o) % PLANE
            arrived(got.at[stream, src], e1.at[stream, src])
        run = jnp.zeros((HD // 2, HD), F32)
        for j in range(PLANE) if stream == KV else reversed(range(PLANE)):
            local[stream, j] = run
            run = run + got[stream, j].astype(F32)
        total[stream] = run.astype(BF16)

    def wanted(stream, here, there):
        return there < here if stream == KV else there > here

    def share(stream):
        for o in range(1, GROUP):
            other = (at + o) % GROUP

            @pl.when(wanted(stream, other, at))
            def _():
                send(total.at[stream], totals.at[stream, at], a2.at[stream, o], e2.at[stream, at], ranked[o - 1])

    def shared(stream):
        for o in range(1, GROUP):
            other = (at + o) % GROUP

            @pl.when(wanted(stream, other, at))
            def _():
                arrived(total.at[stream], a2.at[stream, o])

    def answer(stream):
        for j in range(GROUP):
            @pl.when(wanted(stream, at, j))
            def _():
                arrived(totals.at[stream, j], e2.at[stream, j])

            @pl.when(jnp.logical_not(wanted(stream, at, j)))
            def _():
                totals[stream, j] = jnp.zeros((HD // 2, HD), BF16)
        base = totals[stream, 0].astype(F32)
        for j in range(1, GROUP):
            base = base + totals[stream, j].astype(F32)
        for j in range(PLANE):
            back[stream, j] = (local[stream, j] + base).astype(BF16)
        for o in range(1, PLANE):
            to = (p + o) % PLANE
            sent.append(send(back.at[stream, to], final.at[stream, p], a3.at[stream, o], e3.at[stream, p], plane[o - 1]))
        final[stream, p] = back[stream, p]

    def answered(stream):
        for o in range(1, PLANE):
            src = (p + PLANE - o) % PLANE
            arrived(final.at[stream, src], e3.at[stream, src])

    rows = lax.broadcasted_iota(jnp.int32, (HALF, HALF), 0)
    lanes = lax.broadcasted_iota(jnp.int32, (HALF, HALF), 1)
    causal = rows >= lanes

    def bands(step):
        top = pl.multiple_of((step // H) * BLK, BLK)
        return pl.ds(top, HALF), pl.ds(pl.multiple_of(top + HALF, HALF), HALF), head_cols(step % H)

    def key_side(step):
        top, low, cols = bands(step)
        g0, g1, v0, v1 = g[top, cols], g[low, cols], v[top, cols], v[low, cols]
        s00 = jnp.where(causal, nt(g0, v0), 0.0).astype(BF16)
        s10 = nt(g1, v0).astype(BF16)
        s11 = jnp.where(causal, nt(g1, v1), 0.0).astype(BF16)
        scores[step, 0], scores[step, 1], scores[step, 2] = s00, s10, s11
        q0, q1 = q[top, cols], q[low, cols]
        ki[top, cols] = (tn(s00, q0) + tn(s10, q1)).astype(BF16)
        ki[low, cols] = tn(s11, q1).astype(BF16)

    def state_of(stream, h):
        return final[stream, pl.ds(2 * h, 2)].reshape(HD, HD)

    def key_end(step):
        top, low, cols = bands(step)
        h = step % H
        state = (state_of(QG, h).astype(F32) + jnp.where(step < H, qg1[h].astype(F32), 0.0)).astype(BF16)
        for band in (top, low):
            dk[band, cols] = ((ki[band, cols].astype(F32) + nn(v[band, cols], state)) * att_scale).astype(BF16)

    def query_end(step):
        top, low, cols = bands(step)
        h = step % H
        state = (state_of(KV, h).astype(F32) + jnp.where(step >= H, kv0[h], 0.0)).astype(BF16)
        k0, k1 = k[top, cols], k[low, cols]
        dq[top, cols] = ((nn(scores[step, 0], k0) + nt(g[top, cols], state)) * att_scale).astype(BF16)
        dq[low, cols] = (
            (nn(scores[step, 1], k0) + nn(scores[step, 2], k1) + nt(g[low, cols], state)) * att_scale
        ).astype(BF16)

    def band_and_pair(step, half):
        pair = half * 2 + step % 2
        return pl.ds(pl.multiple_of((step // 2) * 256, 256), 256), pl.ds(pl.multiple_of(pair * 256, 256), 256), pair

    def before_scan(half, whole):
        def body(step):
            band, cols, pair = band_and_pair(step, half)
            upper = nn(xt[band, 0:BLK], v[0:BLK, cols])
            lower = nn(xt[band, BLK : 2 * BLK], v[BLK : 2 * BLK, cols])
            xv[band, cols] = (upper + lower).astype(BF16)
            known = nn(upper.astype(BF16), diagonal(qg1[2 * pair], qg1[2 * pair + 1]))
            if whole:
                known = known + nn(xt[band, :], ki[:, cols])
            pre[band, cols] = known

        return body

    def rest_of(half):
        def body(step):
            band, cols, pair = band_and_pair(step, half)
            pre[band, cols] = pre[band, cols] + nn(xt[band, :], ki[:, cols])

        return body

    def after_scan(half, color, keep):
        pair = half * 2 + color
        cols = pl.ds(pl.multiple_of(pair * 256, 256), 256)
        state = diagonal(state_of(QG, 2 * pair), state_of(QG, 2 * pair + 1))

        @pl.loop(0, 4, unroll=2)
        def _(m):
            band = pl.ds(pl.multiple_of(m * 256, 256), 256)
            made = (pre[band, cols] + nn(xv[band, cols], state)) * (att_scale * grad_scale)
            hi = m // 2
            for part in range(8):
                in_y, in_x = (m % 2) * 2 + part // 4, part % 4
                for lo in range(2):
                    piece = made[part * 32 : part * 32 + 32, lo * 128 : lo * 128 + 128].astype(keep.dtype)
                    if color == 0:
                        keep[color, in_x, in_y, hi, lo] = piece
                    else:
                        keep[color, in_y, in_x, hi, lo] = piece

    loads[0].wait()
    loads[1].wait()
    states(QG, g, q, qg1, 1)
    pl.semaphore_wait(barrier, len(peers))
    spread(QG)
    loads[2].wait()
    loads[3].wait()
    states(KV, k, v, kv0, 0)
    spread(KV)
    loads[4].wait()
    pl.loop(0, N1, unroll=2)(key_side)
    gather(QG)
    share(QG)
    pl.loop(N1, N2, unroll=2)(key_side)
    gather(KV)
    share(KV)
    answer(QG)

    @pl.loop(0, 4)
    def _(m):
        band = pl.ds(pl.multiple_of(m * 256, 256), 256)
        xt[band, :] = x[:, band].T

    pl.loop(N2, 16, unroll=2)(key_side)
    answer(KV)
    pl.loop(0, 8, unroll=2)(before_scan(1 - core, True))
    pl.loop(0, 8, unroll=2)(before_scan(core, False))
    answered(QG)

    for color in range(2):
        after_scan(1 - core, color, give)
        sent.append(send(give.at[color], r0.at[color], s0.at[color], q0.at[color], partner))
    pl.loop(0, 8, unroll=2)(rest_of(core))
    for color in range(2):
        after_scan(core, color, mine)

    lines = ((at_x, along_x), (at_y, along_y))
    def ahead(color, n, to, rows, peer, relay=None):
        part = mine[color, to, rows] + r0[color, to, rows].astype(F32)
        if relay is not None:
            arrived(r1.at[color, relay], q1.at[color, relay])
            part = part + r1[color, relay].astype(F32)
        b[color, n] = part.astype(BF16)
        sent.append(send(b.at[color, n], r1.at[color, n], s1.at[color, n], q1.at[color, n], peer))

    first, second = slice(0, 2), slice(2, 4)
    for color in range(2):
        here, line = lines[color]
        arrived(r0.at[color], q0.at[color])
        up, across, down = (here + 1) % 4, (here + 2) % 4, (here + 3) % 4
        ahead(color, 0, across, first, line[0])
        ahead(color, 1, across, second, line[2])
        ahead(color, 2, up, second, line[0])
        ahead(color, 4, down, first, line[2])
        mine[color, here] = mine[color, here] + r0[color, here].astype(F32)
    pl.loop(0, K1, unroll=2)(key_end)
    for color in range(2):
        here, line = lines[color]
        ahead(color, 3, (here + 1) % 4, first, line[0], 0)
        ahead(color, 5, (here + 3) % 4, second, line[2], 1)
    pl.loop(K1, 16, unroll=2)(key_end)
    outs = []
    copy = pltpu.make_async_copy(dk, dk_hbm, out_sem.at[16])
    copy.start()
    outs.append(copy)
    answered(KV)
    pl.loop(0, M1, unroll=2)(query_end)
    for color in range(2):
        here = lines[color][0]
        there, line = lines[1 - color]
        for n in range(2, 6):
            arrived(r1.at[color, n], q1.at[color, n])
        mine[color, here, first] = mine[color, here, first] + r1[color, 3].astype(F32) + r1[color, 4].astype(F32)
        mine[color, here, second] = mine[color, here, second] + r1[color, 2].astype(F32) + r1[color, 5].astype(F32)
        for o in (2, 1, 3):
            to = (there + o) % 4
            c[color, o] = mine[color, here, to].astype(BF16)
            sent.append(send(c.at[color, o], r2.at[color, o], s2.at[color, o], q2.at[color, o], line[o - 1]))
    for color in range(2):
        here, there = lines[color][0], lines[1 - color][0]
        for o in range(1, 4):
            arrived(r2.at[color, o], q2.at[color, o])
        done[:, color] = (
            mine[color, here, there] + r2[color, 1].astype(F32) + r2[color, 2].astype(F32) + r2[color, 3].astype(F32)
        )
    w[...] = done[...].astype(BF16)
    for o in (2, 1, 3):
        to = (z + o) % 4
        peer = ((to % 2) * 2 + core, (to // 2) * PLANE + p)
        sent.append(send(w.at[to // 2], r3.at[o], s3.at[o], q3.at[o], peer))
    for o in range(1, 4):
        arrived(r3.at[o], q3.at[o])
    summed[...] = done[z_hi] + r3[1].astype(F32) + r3[2].astype(F32) + r3[3].astype(F32)
    fresh = []
    for t in range(4):
        cols = pl.ds(pl.multiple_of(core * 512 + t * 128, 128), 128)
        grad = summed[t // 2, t % 2]
        grad_ref[:, cols] = grad
        fresh.append(adam(grad, master[:, cols], m1[:, cols], m2[:, cols])[0].astype(BF16))

    for color in range(2):
        here, there = lines[color][0], lines[1 - color][0]
        for lo in range(2):
            t = color * 2 + lo
            wide[color, here, z_hi, there, :, lo * 128 : lo * 128 + 128] = fresh[t]
    for color in range(2):
        here, there = lines[color][0], lines[1 - color][0]
        line = lines[1 - color][1]
        near = near_y if color == 0 else near_x
        spot = wide.at[color, here, z_hi, there]
        for o in (2, 1, 3, 0):
            if o:
                sent.append(send(spot, spot, s4.at[color, 0, o], q4.at[color, 0, o], line[o - 1]))
            sent.append(send(spot, spot, s4.at[color, 1, o], q4.at[color, 1, o], near[o]))
    sent.append(send(summed, other_sum, pair_sem.at[0], pair_sem.at[1], partner))
    def onward(color, n, src, hi, peer):
        spot = wide.at[color, src, hi]
        sent.append(send(spot, spot, s5.at[color, n], q5.at[color, n], peer))

    for near in range(2):
        hi = (z_hi + near) % 2
        for color in range(2):
            here, there = lines[color][0], lines[1 - color][0]
            line = lines[color][1]
            for o in range(near == 0, 4):
                arrived(wide.at[color, here, hi, (there + 4 - o) % 4], q4.at[color, near, o])
            onward(color, 2 * near, here, hi, line[2 * near])
            onward(color, 2 * near + 1, here, hi, line[2 - 2 * near])
    for color in range(2):
        here = lines[color][0]
        sent.append(send(wide.at[color, here], far.at[color, here], s6.at[color, 0], q6.at[color, 0], partner))

    def put(src, half, color, at, n):
        cols = pl.ds(pl.multiple_of(half * 512 + color * 256, 256), 256)
        dst = w_hbm.at[:, :, at, :, cols] if color == 0 else w_hbm.at[:, at, :, :, cols]
        copy = pltpu.make_async_copy(src, dst, out_sem.at[n])
        copy.start()
        outs.append(copy)

    pl.loop(M1, M2, unroll=2)(query_end)
    for color in range(2):
        here, line = lines[color]
        put(wide.at[color, here], core, color, here, color * 8)
        arrived(wide.at[color, (here + 3) % 4, z_hi], q5.at[color, 0])
        onward(color, 4, (here + 3) % 4, z_hi, line[0])
    for color in range(2):
        here, line = lines[color]
        arrived(wide.at[color, (here + 1) % 4, 1 - z_hi], q5.at[color, 2])
        onward(color, 5, (here + 1) % 4, 1 - z_hi, line[2])
    pl.loop(M2, 16, unroll=2)(query_end)
    copy = pltpu.make_async_copy(dq, dq_hbm, out_sem.at[17])
    copy.start()
    outs.append(copy)
    for o in (1, 3, 2):
        for color in range(2):
            here = lines[color][0]
            src = (here + 4 - o) % 4
            if o == 1:
                arrived(wide.at[color, src, 1 - z_hi], q5.at[color, 3])
            if o == 3:
                arrived(wide.at[color, src, z_hi], q5.at[color, 1])
            if o == 2:
                arrived(wide.at[color, src, z_hi], q5.at[color, 4])
                arrived(wide.at[color, src, 1 - z_hi], q5.at[color, 5])
            sent.append(send(wide.at[color, src], far.at[color, src], s6.at[color, o], q6.at[color, o], partner))
            put(wide.at[color, src], core, color, src, color * 8 + o)
    for o in (0, 1, 3, 2):
        for color in range(2):
            here = lines[color][0]
            src = (here + 4 - o) % 4
            arrived(far.at[color, src], q6.at[color, o])
            put(far.at[color, src], 1 - core, color, src, color * 8 + 4 + o)
    arrived(other_sum, pair_sem.at[1])
    for t in range(4):
        cols = pl.ds(pl.multiple_of((1 - core) * 512 + t * 128, 128), 128)
        grad_ref[:, cols] = other_sum[t // 2, t % 2]
    for copy in sent:
        copy.wait_send()
    shared(QG)
    shared(KV)
    for copy in outs:
        copy.wait()


def kernel_call(att_scale, grad_scale, inputs, q, k, v, g, master, m1, m2):
    width = inputs.shape[1]
    dma = pltpu.SemaphoreType.DMA
    tile = (32, 128)
    piece = (HD // 2, HD)
    wide = (2, 4, 2, 4, 32, 256)
    big = pltpu.VMEM(q.shape, BF16)
    full = jax.ShapeDtypeStruct(q.shape, BF16)
    return pl.pallas_call(
        lambda *refs: kernel(att_scale, grad_scale, *refs),
        out_shape=(full, full, jax.ShapeDtypeStruct((2, 4, 4, 32, width), BF16), jax.ShapeDtypeStruct(master.shape, F32)),
        in_specs=[ANY] * 5 + [VMEM] * 3,
        out_specs=(ANY, ANY, ANY, VMEM),
        scratch_shapes=[
            big, big, big, big, big, big, big, big, big, big,
            pltpu.VMEM((width, width), F32),
            pltpu.VMEM((2 * H, 3, HALF, HALF), BF16),
            pltpu.VMEM((H, HD, HD), BF16),
            pltpu.VMEM((H, HD, HD), F32),
            pltpu.VMEM((2, PLANE) + piece, BF16),
            pltpu.VMEM((2, PLANE) + piece, BF16),
            pltpu.VMEM((2, PLANE) + piece, F32),
            pltpu.VMEM((2,) + piece, BF16),
            pltpu.VMEM((2, GROUP) + piece, BF16),
            pltpu.VMEM((2, PLANE) + piece, BF16),
            pltpu.VMEM((2, PLANE) + piece, BF16),
            pltpu.VMEM((2, 4, 4, 2, 2) + tile, BF16),
            pltpu.VMEM((2, 4, 4, 2, 2) + tile, F32),
            pltpu.VMEM((2, 4, 4, 2, 2) + tile, BF16),
            pltpu.VMEM((2, 6, 2, 2, 2) + tile, BF16),
            pltpu.VMEM((2, 6, 2, 2, 2) + tile, BF16),
            pltpu.VMEM((2, 4, 2, 2) + tile, BF16),
            pltpu.VMEM((2, 4, 2, 2) + tile, BF16),
            pltpu.VMEM((4, 2, 2) + tile, BF16),
            pltpu.VMEM((2, 2, 2) + tile, BF16),
            pltpu.VMEM((2, 2, 2) + tile, F32),
            pltpu.VMEM((2, 2) + tile, F32),
            pltpu.VMEM((2, 2) + tile, F32),
            pltpu.VMEM(wide, BF16),
            pltpu.VMEM(wide, BF16),
            dma((5,)), dma((18,)),
            dma((2, PLANE)), dma((2, PLANE)), dma((2, GROUP)), dma((2, GROUP)), dma((2, PLANE)), dma((2, PLANE)),
            dma((2,)), dma((2,)), dma((2, 6)), dma((2, 6)), dma((2, 4)), dma((2, 4)),
            dma((4,)), dma((4,)), dma((2, 2, 4)), dma((2, 2, 4)),
            dma((2, 6)), dma((2, 6)), dma((2, 4)), dma((2, 4)), dma((2,)),
        ],
        compiler_params=pltpu.CompilerParams(collective_id=0, has_side_effects=True, vmem_limit_bytes=56 << 20),
        name="backward",
    )(inputs, q, k, v, g, master, m1, m2)


def local(inputs, queries, keys, values, out_grad, master, moment1, moment2):
    total_tokens = inputs.shape[0] * lax.axis_size("outer") * lax.axis_size("inner")
    att_scale = 1.0 / math.sqrt(HD * total_tokens)
    grad_scale = 1.0 / math.sqrt(total_tokens)
    query_grad, key_grad, weights, grad = kernel_call(
        att_scale, grad_scale, inputs, queries, keys, values, out_grad, master, moment1, moment2
    )
    new_master, first, second = adam(grad, master, moment1, moment2)
    return query_grad, key_grad, new_master, first, second, weights.reshape(inputs.shape[1], -1)


def solution(mesh):
    tokens, shard = P(("outer", "inner"), None), P("inner", None)
    return jax.shard_map(
        local,
        mesh=mesh,
        in_specs=(tokens,) * 5 + (shard,) * 3,
        out_specs=(tokens, tokens, shard, shard, shard, P()),
        check_vma=False,
    )
```

```python
import math

import jax
import jax.numpy as jnp
from jax import lax
from jax.experimental import pallas as pl
from jax.experimental.pallas import tpu as pltpu
from jax.sharding import PartitionSpec as P

H = 8
HD = 128
BLK = 512
HALF = BLK // 2
PLANE = 16
N1, N2, M1, M2, VM = 6, 10, 4, 10, 47
GROUP = 8
MESH = pl.DeviceIdType.MESH
F32 = jnp.float32
BF16 = jnp.bfloat16
ANY = pl.BlockSpec(memory_space=pl.ANY)
HBM = pl.BlockSpec(memory_space=pltpu.HBM)
VMEM = pl.BlockSpec(memory_space=pltpu.VMEM)


def nt(a, b):
    return lax.dot_general(a, b, (((1,), (1,)), ((), ())), preferred_element_type=F32)


def tn(a, b):
    return lax.dot_general(a, b, (((0,), (0,)), ((), ())), preferred_element_type=F32)


def nn(a, b):
    return lax.dot_general(a, b, (((1,), (0,)), ((), ())), preferred_element_type=F32)


def place():
    outer, inner = lax.axis_index("outer"), lax.axis_index("inner")
    return outer, inner, outer // 2, outer % 2, inner // PLANE, inner % PLANE


def greet(barrier, peers):
    for peer in peers:
        pl.semaphore_signal(barrier, inc=1, device_id=peer, device_id_type=MESH)


def send(src, dst, send_sem, recv_sem, peer):
    copy = pltpu.make_async_remote_copy(
        src_ref=src, dst_ref=dst, send_sem=send_sem, recv_sem=recv_sem, device_id=peer, device_id_type=MESH
    )
    copy.start()
    return copy


def arrived(ref, sem):
    pltpu.make_async_copy(ref, ref, sem).wait()


def adam(grad, master, m1, m2):
    first = 0.9 * m1 + 0.1 * grad
    second = 0.95 * m2 + 0.05 * grad * grad
    new = master - 0.01 * (first / (jnp.sqrt(second) + 1e-08) + 0.1 * master)
    return new, first, second


def diagonal(first, second):
    zero = jnp.zeros_like(first)
    return jnp.concatenate([jnp.concatenate([first, zero], 1), jnp.concatenate([zero, second], 1)], 0)


def kernel(
    att_scale, grad_scale,
    x_hbm, q_hbm, k_hbm, v_hbm, g_hbm, master_hbm, m1_hbm, m2_hbm,
    dq_hbm, dk_hbm, w_hbm, grad_ref,
    master, m1, m2, x, q, k, v, g, xt, ki, xv, dq, dk, pre, scores, qg1, kv0,
    own, got, local, total, totals, back, final,
    give, mine, r0, r1, b, r2, c, r3, w, done, summed, other_sum, wide, far,
    in_sem, out_sem, a1, e1, a2, e2, a3, e3,
    s0, q0, s1, q1, s2, q2, s3, q3, s4, q4, s5, q5, s6, q6, pair_sem,
):
    outer, inner, z_lo, core, z_hi, p = place()
    at_y, at_x = p // 4, p % 4
    z = z_hi * 2 + z_lo
    at = z_lo * 4 + core * 2 + z_hi
    plane = [(outer, z_hi * PLANE + (p + o) % PLANE) for o in range(1, PLANE)]
    ranked = []
    for o in range(1, GROUP):
        other = (at + o) % GROUP
        ranked.append((other // 2, (other % 2) * PLANE + p))
    partner = (z_lo * 2 + 1 - core, inner)
    along_x = [(outer, z_hi * PLANE + at_y * 4 + (at_x + o) % 4) for o in range(1, 4)]
    along_y = [(outer, z_hi * PLANE + ((at_y + o) % 4) * 4 + at_x) for o in range(1, 4)]
    beside = (z + 4 + 2 * z_lo - 1) % 4
    beside_outer, beside_inner = (beside % 2) * 2 + core, (beside // 2) * PLANE
    near_x = [(beside_outer, beside_inner + at_y * 4 + (at_x + o) % 4) for o in range(4)]
    near_y = [(beside_outer, beside_inner + ((at_y + o) % 4) * 4 + at_x) for o in range(4)]
    peers = plane + ranked + near_x[1:] + near_y[1:]
    barrier = pltpu.get_barrier_semaphore()
    greet(barrier, peers)
    loads = []
    for n, (src, dst) in enumerate(((g_hbm, g), (q_hbm, q), (k_hbm, k), (v_hbm, v), (x_hbm, x), (master_hbm, master), (m1_hbm, m1), (m2_hbm, m2))):
        copy = pltpu.make_async_copy(src, dst, in_sem.at[n])
        copy.start()
        loads.append(copy)
    sent = []
    QG, KV = 0, 1

    def head_cols(h):
        return pl.ds(pl.multiple_of(h * HD, HD), HD)

    def states(stream, left, right, keep, kept):
        @pl.loop(0, H)
        def _(h):
            cols = head_cols(h)
            blocks = [tn(left[n * BLK : (n + 1) * BLK, cols], right[n * BLK : (n + 1) * BLK, cols]) for n in range(2)]
            keep[h] = blocks[kept].astype(keep.dtype)
            both = (blocks[0] + blocks[1]).astype(BF16)
            own[stream, 2 * h] = both[0 : HD // 2]
            own[stream, 2 * h + 1] = both[HD // 2 :]

    def spread(stream):
        for o in range(1, PLANE):
            to = (p + o) % PLANE
            sent.append(send(own.at[stream, to], got.at[stream, p], a1.at[stream, o], e1.at[stream, p], plane[o - 1]))
        got[stream, p] = own[stream, p]

    def gather(stream):
        for o in range(1, PLANE):
            src = (p + PLANE - o) % PLANE
            arrived(got.at[stream, src], e1.at[stream, src])
        run = jnp.zeros((HD // 2, HD), F32)
        for j in range(PLANE) if stream == KV else reversed(range(PLANE)):
            local[stream, j] = run
            run = run + got[stream, j].astype(F32)
        total[stream] = run.astype(BF16)

    def wanted(stream, here, there):
        return there < here if stream == KV else there > here

    def share(stream):
        for o in range(1, GROUP):
            other = (at + o) % GROUP

            @pl.when(wanted(stream, other, at))
            def _():
                send(total.at[stream], totals.at[stream, at], a2.at[stream, o], e2.at[stream, at], ranked[o - 1])

    def shared(stream):
        for o in range(1, GROUP):
            other = (at + o) % GROUP

            @pl.when(wanted(stream, other, at))
            def _():
                arrived(total.at[stream], a2.at[stream, o])

    def answer(stream):
        for j in range(GROUP):
            @pl.when(wanted(stream, at, j))
            def _():
                arrived(totals.at[stream, j], e2.at[stream, j])

            @pl.when(jnp.logical_not(wanted(stream, at, j)))
            def _():
                totals[stream, j] = jnp.zeros((HD // 2, HD), BF16)
        base = totals[stream, 0].astype(F32)
        for j in range(1, GROUP):
            base = base + totals[stream, j].astype(F32)
        for j in range(PLANE):
            back[stream, j] = (local[stream, j] + base).astype(BF16)
        for o in range(1, PLANE):
            to = (p + o) % PLANE
            sent.append(send(back.at[stream, to], final.at[stream, p], a3.at[stream, o], e3.at[stream, p], plane[o - 1]))
        final[stream, p] = back[stream, p]

    def answered(stream):
        for o in range(1, PLANE):
            src = (p + PLANE - o) % PLANE
            arrived(final.at[stream, src], e3.at[stream, src])

    rows = lax.broadcasted_iota(jnp.int32, (HALF, HALF), 0)
    lanes = lax.broadcasted_iota(jnp.int32, (HALF, HALF), 1)
    causal = rows >= lanes

    def bands(step):
        top = pl.multiple_of((step // H) * BLK, BLK)
        return pl.ds(top, HALF), pl.ds(pl.multiple_of(top + HALF, HALF), HALF), head_cols(step % H)

    def key_side(step):
        top, low, cols = bands(step)
        g0, g1, v0, v1 = g[top, cols], g[low, cols], v[top, cols], v[low, cols]
        s00 = jnp.where(causal, nt(g0, v0), 0.0).astype(BF16)
        s10 = nt(g1, v0).astype(BF16)
        s11 = jnp.where(causal, nt(g1, v1), 0.0).astype(BF16)
        scores[step, 0], scores[step, 1], scores[step, 2] = s00, s10, s11
        q0, q1 = q[top, cols], q[low, cols]
        ki[top, cols] = (tn(s00, q0) + tn(s10, q1)).astype(BF16)
        ki[low, cols] = tn(s11, q1).astype(BF16)

    def state_of(stream, h):
        return final[stream, pl.ds(2 * h, 2)].reshape(HD, HD)

    def key_end(step):
        top, low, cols = bands(step)
        h = step % H
        state = (state_of(QG, h).astype(F32) + jnp.where(step < H, qg1[h].astype(F32), 0.0)).astype(BF16)
        for band in (top, low):
            dk[band, cols] = ((ki[band, cols].astype(F32) + nn(v[band, cols], state)) * att_scale).astype(BF16)

    def query_end(step):
        top, low, cols = bands(step)
        h = step % H
        state = (state_of(KV, h).astype(F32) + jnp.where(step >= H, kv0[h], 0.0)).astype(BF16)
        k0, k1 = k[top, cols], k[low, cols]
        dq[top, cols] = ((nn(scores[step, 0], k0) + nt(g[top, cols], state)) * att_scale).astype(BF16)
        dq[low, cols] = (
            (nn(scores[step, 1], k0) + nn(scores[step, 2], k1) + nt(g[low, cols], state)) * att_scale
        ).astype(BF16)

    def before_scan(step):
        pair = (1 - core) * 2 + step % 2
        band = pl.ds(pl.multiple_of((step // 2) * 256, 256), 256)
        cols = pl.ds(pl.multiple_of(pair * 256, 256), 256)
        upper = nn(xt[band, 0:BLK], v[0:BLK, cols])
        lower = nn(xt[band, BLK : 2 * BLK], v[BLK : 2 * BLK, cols])
        xv[band, cols] = (upper + lower).astype(BF16)
        pre[band, cols] = nn(xt[band, :], ki[:, cols]) + nn(
            upper.astype(BF16), diagonal(qg1[2 * pair], qg1[2 * pair + 1])
        )

    def lay(made, m, color, keep):
        hi = m // 2
        for part in range(8):
            in_y, in_x = (m % 2) * 2 + part // 4, part % 4
            for lo in range(2):
                piece = made[part * 32 : part * 32 + 32, lo * 128 : lo * 128 + 128].astype(keep.dtype)
                if color == 0:
                    keep[color, in_x, in_y, hi, lo] = piece
                else:
                    keep[color, in_y, in_x, hi, lo] = piece

    def after_scan(color):
        pair = (1 - core) * 2 + color
        cols = pl.ds(pl.multiple_of(pair * 256, 256), 256)
        state = diagonal(state_of(QG, 2 * pair), state_of(QG, 2 * pair + 1))

        def body(m):
            band = pl.ds(pl.multiple_of(m * 256, 256), 256)
            lay((pre[band, cols] + nn(xv[band, cols], state)) * (att_scale * grad_scale), m, color, give)

        return body

    def product(color):
        cols = pl.ds(pl.multiple_of((core * 2 + color) * 256, 256), 256)

        def body(m):
            band = pl.ds(pl.multiple_of(m * 256, 256), 256)
            lay(nn(xt[band, :], dk[:, cols]) * grad_scale, m, color, mine)

        return body

    def key_pair(half, color):
        return lambda step: key_end((step // 2) * H + half * 4 + color * 2 + step % 2)

    loads[0].wait()
    loads[1].wait()
    states(QG, g, q, qg1, 1)
    pl.semaphore_wait(barrier, len(peers))
    spread(QG)
    loads[2].wait()
    loads[3].wait()
    states(KV, k, v, kv0, 0)
    loads[4].wait()
    pl.loop(0, N1, unroll=2)(key_side)
    gather(QG)
    share(QG)
    spread(KV)
    pl.loop(N1, N2, unroll=2)(key_side)
    answer(QG)

    @pl.loop(0, 4)
    def _(m):
        band = pl.ds(pl.multiple_of(m * 256, 256), 256)
        xt[band, :] = x[:, band].T

    pl.loop(N2, 16, unroll=2)(key_side)
    gather(KV)
    share(KV)
    pl.loop(0, 8, unroll=2)(before_scan)
    answered(QG)

    for color in range(2):
        pl.loop(0, 4, unroll=2)(after_scan(color))
        sent.append(send(give.at[color], r0.at[color], s0.at[color], q0.at[color], partner))
    answer(KV)

    lines = ((at_x, along_x), (at_y, along_y))
    def ahead(color, n, to, rows, peer, relay=None):
        part = mine[color, to, rows] + r0[color, to, rows].astype(F32)
        if relay is not None:
            arrived(r1.at[color, relay], q1.at[color, relay])
            part = part + r1[color, relay].astype(F32)
        b[color, n] = part.astype(BF16)
        sent.append(send(b.at[color, n], r1.at[color, n], s1.at[color, n], q1.at[color, n], peer))

    first, second = slice(0, 2), slice(2, 4)
    for color in range(2):
        here, line = lines[color]
        pl.loop(0, 4, unroll=2)(key_pair(core, color))
        pl.loop(0, 4, unroll=2)(product(color))
        arrived(r0.at[color], q0.at[color])
        up, across, down = (here + 1) % 4, (here + 2) % 4, (here + 3) % 4
        ahead(color, 0, across, first, line[0])
        ahead(color, 1, across, second, line[2])
        ahead(color, 2, up, second, line[0])
        ahead(color, 4, down, first, line[2])
        mine[color, here] = mine[color, here] + r0[color, here].astype(F32)
    for color in range(2):
        here, line = lines[color]
        ahead(color, 3, (here + 1) % 4, first, line[0], 0)
        ahead(color, 5, (here + 3) % 4, second, line[2], 1)
        pl.loop(0, 4, unroll=2)(key_pair(1 - core, color))
    outs = []
    copy = pltpu.make_async_copy(dk, dk_hbm, out_sem.at[16])
    copy.start()
    outs.append(copy)
    answered(KV)
    pl.loop(0, M1, unroll=2)(query_end)
    for color in range(2):
        here = lines[color][0]
        there, line = lines[1 - color]
        for n in range(2, 6):
            arrived(r1.at[color, n], q1.at[color, n])
        mine[color, here, first] = mine[color, here, first] + r1[color, 3].astype(F32) + r1[color, 4].astype(F32)
        mine[color, here, second] = mine[color, here, second] + r1[color, 2].astype(F32) + r1[color, 5].astype(F32)
        for o in (2, 1, 3):
            to = (there + o) % 4
            c[color, o] = mine[color, here, to].astype(BF16)
            sent.append(send(c.at[color, o], r2.at[color, o], s2.at[color, o], q2.at[color, o], line[o - 1]))
    for color in range(2):
        here, there = lines[color][0], lines[1 - color][0]
        for o in range(1, 4):
            arrived(r2.at[color, o], q2.at[color, o])
        done[:, color] = (
            mine[color, here, there] + r2[color, 1].astype(F32) + r2[color, 2].astype(F32) + r2[color, 3].astype(F32)
        )
    w[...] = done[...].astype(BF16)
    for o in (2, 1, 3):
        to = (z + o) % 4
        peer = ((to % 2) * 2 + core, (to // 2) * PLANE + p)
        sent.append(send(w.at[to // 2], r3.at[o], s3.at[o], q3.at[o], peer))
    for o in range(1, 4):
        arrived(r3.at[o], q3.at[o])
    for load in loads[5:]:
        load.wait()
    summed[...] = done[z_hi] + r3[1].astype(F32) + r3[2].astype(F32) + r3[3].astype(F32)
    fresh = []
    for t in range(4):
        cols = pl.ds(pl.multiple_of(core * 512 + t * 128, 128), 128)
        grad = summed[t // 2, t % 2]
        grad_ref[:, cols] = grad
        fresh.append(adam(grad, master[:, cols], m1[:, cols], m2[:, cols])[0].astype(BF16))

    for color in range(2):
        here, there = lines[color][0], lines[1 - color][0]
        for lo in range(2):
            t = color * 2 + lo
            wide[color, here, z_hi, there, :, lo * 128 : lo * 128 + 128] = fresh[t]
    for color in range(2):
        here, there = lines[color][0], lines[1 - color][0]
        line = lines[1 - color][1]
        near = near_y if color == 0 else near_x
        spot = wide.at[color, here, z_hi, there]
        for o in (2, 1, 3, 0):
            if o:
                sent.append(send(spot, spot, s4.at[color, 0, o], q4.at[color, 0, o], line[o - 1]))
            sent.append(send(spot, spot, s4.at[color, 1, o], q4.at[color, 1, o], near[o]))
    sent.append(send(summed, other_sum, pair_sem.at[0], pair_sem.at[1], partner))
    def onward(color, n, src, hi, peer):
        spot = wide.at[color, src, hi]
        sent.append(send(spot, spot, s5.at[color, n], q5.at[color, n], peer))

    for near in range(2):
        hi = (z_hi + near) % 2
        for color in range(2):
            here, there = lines[color][0], lines[1 - color][0]
            line = lines[color][1]
            for o in range(near == 0, 4):
                arrived(wide.at[color, here, hi, (there + 4 - o) % 4], q4.at[color, near, o])
            onward(color, 2 * near, here, hi, line[2 * near])
            onward(color, 2 * near + 1, here, hi, line[2 - 2 * near])
    for color in range(2):
        here = lines[color][0]
        sent.append(send(wide.at[color, here], far.at[color, here], s6.at[color, 0], q6.at[color, 0], partner))

    def put(src, half, color, at, n):
        cols = pl.ds(pl.multiple_of(half * 512 + color * 256, 256), 256)
        dst = w_hbm.at[:, :, at, :, cols] if color == 0 else w_hbm.at[:, at, :, :, cols]
        copy = pltpu.make_async_copy(src, dst, out_sem.at[n])
        copy.start()
        outs.append(copy)

    pl.loop(M1, M2, unroll=2)(query_end)
    for color in range(2):
        here, line = lines[color]
        put(wide.at[color, here], core, color, here, color * 8)
        arrived(wide.at[color, (here + 3) % 4, z_hi], q5.at[color, 0])
        onward(color, 4, (here + 3) % 4, z_hi, line[0])
    for color in range(2):
        here, line = lines[color]
        arrived(wide.at[color, (here + 1) % 4, 1 - z_hi], q5.at[color, 2])
        onward(color, 5, (here + 1) % 4, 1 - z_hi, line[2])
    pl.loop(M2, 16, unroll=2)(query_end)
    copy = pltpu.make_async_copy(dq, dq_hbm, out_sem.at[17])
    copy.start()
    outs.append(copy)
    for o in (1, 3, 2):
        for color in range(2):
            here = lines[color][0]
            src = (here + 4 - o) % 4
            if o == 1:
                arrived(wide.at[color, src, 1 - z_hi], q5.at[color, 3])
            if o == 3:
                arrived(wide.at[color, src, z_hi], q5.at[color, 1])
            if o == 2:
                arrived(wide.at[color, src, z_hi], q5.at[color, 4])
                arrived(wide.at[color, src, 1 - z_hi], q5.at[color, 5])
            sent.append(send(wide.at[color, src], far.at[color, src], s6.at[color, o], q6.at[color, o], partner))
            put(wide.at[color, src], core, color, src, color * 8 + o)
    for o in (0, 1, 3, 2):
        for color in range(2):
            here = lines[color][0]
            src = (here + 4 - o) % 4
            arrived(far.at[color, src], q6.at[color, o])
            put(far.at[color, src], 1 - core, color, src, color * 8 + 4 + o)
    arrived(other_sum, pair_sem.at[1])
    for t in range(4):
        cols = pl.ds(pl.multiple_of((1 - core) * 512 + t * 128, 128), 128)
        grad_ref[:, cols] = other_sum[t // 2, t % 2]
    for copy in sent:
        copy.wait_send()
    shared(QG)
    shared(KV)
    for copy in outs:
        copy.wait()


def kernel_call(att_scale, grad_scale, inputs, q, k, v, g, master, m1, m2):
    width = inputs.shape[1]
    dma = pltpu.SemaphoreType.DMA
    tile = (32, 128)
    piece = (HD // 2, HD)
    wide = (2, 4, 2, 4, 32, 256)
    big = pltpu.VMEM(q.shape, BF16)
    full = jax.ShapeDtypeStruct(q.shape, BF16)
    return pl.pallas_call(
        lambda *refs: kernel(att_scale, grad_scale, *refs),
        out_shape=(full, full, jax.ShapeDtypeStruct((2, 4, 4, 32, width), BF16), jax.ShapeDtypeStruct(master.shape, F32)),
        in_specs=[HBM] * 8,
        out_specs=(ANY, ANY, ANY, VMEM),
        scratch_shapes=[
            pltpu.VMEM(master.shape, F32), pltpu.VMEM(master.shape, F32), pltpu.VMEM(master.shape, F32),
            big, big, big, big, big, big, big, big, big, big,
            pltpu.VMEM((width, width), F32),
            pltpu.VMEM((2 * H, 3, HALF, HALF), BF16),
            pltpu.VMEM((H, HD, HD), BF16),
            pltpu.VMEM((H, HD, HD), F32),
            pltpu.VMEM((2, PLANE) + piece, BF16),
            pltpu.VMEM((2, PLANE) + piece, BF16),
            pltpu.VMEM((2, PLANE) + piece, F32),
            pltpu.VMEM((2,) + piece, BF16),
            pltpu.VMEM((2, GROUP) + piece, BF16),
            pltpu.VMEM((2, PLANE) + piece, BF16),
            pltpu.VMEM((2, PLANE) + piece, BF16),
            pltpu.VMEM((2, 4, 4, 2, 2) + tile, BF16),
            pltpu.VMEM((2, 4, 4, 2, 2) + tile, F32),
            pltpu.VMEM((2, 4, 4, 2, 2) + tile, BF16),
            pltpu.VMEM((2, 6, 2, 2, 2) + tile, BF16),
            pltpu.VMEM((2, 6, 2, 2, 2) + tile, BF16),
            pltpu.VMEM((2, 4, 2, 2) + tile, BF16),
            pltpu.VMEM((2, 4, 2, 2) + tile, BF16),
            pltpu.VMEM((4, 2, 2) + tile, BF16),
            pltpu.VMEM((2, 2, 2) + tile, BF16),
            pltpu.VMEM((2, 2, 2) + tile, F32),
            pltpu.VMEM((2, 2) + tile, F32),
            pltpu.VMEM((2, 2) + tile, F32),
            pltpu.VMEM(wide, BF16),
            pltpu.VMEM(wide, BF16),
            dma((8,)), dma((18,)),
            dma((2, PLANE)), dma((2, PLANE)), dma((2, GROUP)), dma((2, GROUP)), dma((2, PLANE)), dma((2, PLANE)),
            dma((2,)), dma((2,)), dma((2, 6)), dma((2, 6)), dma((2, 4)), dma((2, 4)),
            dma((4,)), dma((4,)), dma((2, 2, 4)), dma((2, 2, 4)),
            dma((2, 6)), dma((2, 6)), dma((2, 4)), dma((2, 4)), dma((2,)),
        ],
        compiler_params=pltpu.CompilerParams(collective_id=0, has_side_effects=True, vmem_limit_bytes=VM << 20),
        name="backward",
    )(*[pltpu.with_memory_space_constraint(a, pltpu.HBM) for a in (inputs, q, k, v, g, master, m1, m2)])


def local(inputs, queries, keys, values, out_grad, master, moment1, moment2):
    total_tokens = inputs.shape[0] * lax.axis_size("outer") * lax.axis_size("inner")
    att_scale = 1.0 / math.sqrt(HD * total_tokens)
    grad_scale = 1.0 / math.sqrt(total_tokens)
    query_grad, key_grad, weights, grad = kernel_call(
        att_scale, grad_scale, inputs, queries, keys, values, out_grad, master, moment1, moment2
    )
    new_master, first, second = adam(grad, master, moment1, moment2)
    return query_grad, key_grad, new_master, first, second, weights.reshape(inputs.shape[1], -1)


def solution(mesh):
    tokens, shard = P(("outer", "inner"), None), P("inner", None)
    return jax.shard_map(
        local,
        mesh=mesh,
        in_specs=(tokens,) * 5 + (shard,) * 3,
        out_specs=(tokens, tokens, shard, shard, shard, P()),
        check_vma=False,
    )
```

```python
import math

import jax
import jax.numpy as jnp
from jax import lax
from jax.experimental import pallas as pl
from jax.experimental.pallas import tpu as pltpu
from jax.sharding import PartitionSpec as P

H = 8
HD = 128
BLK = 512
HALF = BLK // 2
PLANE = 16
N1, N2, M1, M2, M3, VM = 6, 10, 8, 10, 12, 47
GROUP = 8
MESH = pl.DeviceIdType.MESH
F32 = jnp.float32
BF16 = jnp.bfloat16
ANY = pl.BlockSpec(memory_space=pl.ANY)
HBM = pl.BlockSpec(memory_space=pltpu.HBM)
VMEM = pl.BlockSpec(memory_space=pltpu.VMEM)


def nt(a, b):
    return lax.dot_general(a, b, (((1,), (1,)), ((), ())), preferred_element_type=F32)


def tn(a, b):
    return lax.dot_general(a, b, (((0,), (0,)), ((), ())), preferred_element_type=F32)


def nn(a, b):
    return lax.dot_general(a, b, (((1,), (0,)), ((), ())), preferred_element_type=F32)


def place():
    outer, inner = lax.axis_index("outer"), lax.axis_index("inner")
    return outer, inner, outer // 2, outer % 2, inner // PLANE, inner % PLANE


def greet(barrier, peers):
    for peer in peers:
        pl.semaphore_signal(barrier, inc=1, device_id=peer, device_id_type=MESH)


def send(src, dst, send_sem, recv_sem, peer):
    copy = pltpu.make_async_remote_copy(
        src_ref=src, dst_ref=dst, send_sem=send_sem, recv_sem=recv_sem, device_id=peer, device_id_type=MESH
    )
    copy.start()
    return copy


def arrived(ref, sem):
    pltpu.make_async_copy(ref, ref, sem).wait()


def adam(grad, master, m1, m2):
    first = 0.9 * m1 + 0.1 * grad
    second = 0.95 * m2 + 0.05 * grad * grad
    new = master - 0.01 * (first / (jnp.sqrt(second) + 1e-08) + 0.1 * master)
    return new, first, second


def diagonal(first, second):
    zero = jnp.zeros_like(first)
    return jnp.concatenate([jnp.concatenate([first, zero], 1), jnp.concatenate([zero, second], 1)], 0)


def kernel(
    att_scale, grad_scale,
    x_hbm, q_hbm, k_hbm, v_hbm, g_hbm, master_hbm, m1_hbm, m2_hbm,
    dq_hbm, dk_hbm, w_hbm, grad_ref,
    master, m1, m2, x, q, k, v, g, xt, ki, xv, dq, dk, pre, scores, qg1, kv0,
    own, got, local, total, totals, back, final,
    give, mine, r0, r1, b, r2, c, r3, w, done, summed, other_sum, wide, far,
    in_sem, out_sem, a1, e1, a2, e2, a3, e3,
    s0, q0, s1, q1, s2, q2, s3, q3, s4, q4, s5, q5, s6, q6, pair_sem,
):
    outer, inner, z_lo, core, z_hi, p = place()
    at_y, at_x = p // 4, p % 4
    z = z_hi * 2 + z_lo
    at = z_lo * 4 + core * 2 + z_hi
    plane = [(outer, z_hi * PLANE + (p + o) % PLANE) for o in range(1, PLANE)]
    ranked = []
    for o in range(1, GROUP):
        other = (at + o) % GROUP
        ranked.append((other // 2, (other % 2) * PLANE + p))
    partner = (z_lo * 2 + 1 - core, inner)
    along_x = [(outer, z_hi * PLANE + at_y * 4 + (at_x + o) % 4) for o in range(1, 4)]
    along_y = [(outer, z_hi * PLANE + ((at_y + o) % 4) * 4 + at_x) for o in range(1, 4)]
    beside = (z + 4 + 2 * z_lo - 1) % 4
    beside_outer, beside_inner = (beside % 2) * 2 + core, (beside // 2) * PLANE
    near_x = [(beside_outer, beside_inner + at_y * 4 + (at_x + o) % 4) for o in range(4)]
    near_y = [(beside_outer, beside_inner + ((at_y + o) % 4) * 4 + at_x) for o in range(4)]
    far_first = (10, 6, 9, 11, 5, 7, 13, 14, 15, 1, 2, 3, 8, 4, 12)
    peers = [plane[o - 1] for o in far_first] + near_x[1:] + near_y[1:] + ranked
    barrier = pltpu.get_barrier_semaphore()
    loads = []

    def load(*pairs):
        for src, dst in pairs:
            copy = pltpu.make_async_copy(src, dst, in_sem.at[len(loads)])
            copy.start()
            loads.append(copy)

    for side in range(2):
        cols = slice(side * H // 2 * HD, (side + 1) * H // 2 * HD)
        load((g_hbm.at[:, cols], g.at[:, cols]), (q_hbm.at[:, cols], q.at[:, cols]))
    greet(barrier, peers)
    sent = []
    QG, KV = 0, 1

    def head_cols(h):
        return pl.ds(pl.multiple_of(h * HD, HD), HD)

    def states(stream, left, right, keep, kept, heads):
        @pl.loop(*heads, unroll=2)
        def _(h):
            cols = head_cols(h)
            blocks = [tn(left[n * BLK : (n + 1) * BLK, cols], right[n * BLK : (n + 1) * BLK, cols]) for n in range(2)]
            keep[h] = blocks[kept].astype(keep.dtype)
            both = (blocks[0] + blocks[1]).astype(BF16)
            own[stream, 2 * h] = both[0 : HD // 2]
            own[stream, 2 * h + 1] = both[HD // 2 :]

    def spread(stream):
        for o in range(1, PLANE):
            to = (p + o) % PLANE
            sent.append(send(own.at[stream, to], got.at[stream, p], a1.at[stream, o], e1.at[stream, p], plane[o - 1]))
        got[stream, p] = own[stream, p]

    def gather(stream):
        for o in range(1, PLANE):
            src = (p + PLANE - o) % PLANE
            arrived(got.at[stream, src], e1.at[stream, src])
        run = jnp.zeros((HD // 2, HD), F32)
        for j in range(PLANE) if stream == KV else reversed(range(PLANE)):
            local[stream, j] = run
            run = run + got[stream, j].astype(F32)
        total[stream] = run.astype(BF16)

    def wanted(stream, here, there):
        return there < here if stream == KV else there > here

    def share(stream):
        for o in range(1, GROUP):
            other = (at + o) % GROUP

            @pl.when(wanted(stream, other, at))
            def _():
                send(total.at[stream], totals.at[stream, at], a2.at[stream, o], e2.at[stream, at], ranked[o - 1])

    def shared(stream):
        for o in range(1, GROUP):
            other = (at + o) % GROUP

            @pl.when(wanted(stream, other, at))
            def _():
                arrived(total.at[stream], a2.at[stream, o])

    def answer(stream):
        for j in range(GROUP):
            @pl.when(wanted(stream, at, j))
            def _():
                arrived(totals.at[stream, j], e2.at[stream, j])

            @pl.when(jnp.logical_not(wanted(stream, at, j)))
            def _():
                totals[stream, j] = jnp.zeros((HD // 2, HD), BF16)
        base = totals[stream, 0].astype(F32)
        for j in range(1, GROUP):
            base = base + totals[stream, j].astype(F32)
        for j in range(PLANE):
            back[stream, j] = (local[stream, j] + base).astype(BF16)
        for o in range(1, PLANE):
            to = (p + o) % PLANE
            sent.append(send(back.at[stream, to], final.at[stream, p], a3.at[stream, o], e3.at[stream, p], plane[o - 1]))
        final[stream, p] = back[stream, p]

    def answered(stream):
        for o in range(1, PLANE):
            src = (p + PLANE - o) % PLANE
            arrived(final.at[stream, src], e3.at[stream, src])

    rows = lax.broadcasted_iota(jnp.int32, (HALF, HALF), 0)
    lanes = lax.broadcasted_iota(jnp.int32, (HALF, HALF), 1)
    causal = rows >= lanes

    def bands(step):
        top = pl.multiple_of((step // H) * BLK, BLK)
        return pl.ds(top, HALF), pl.ds(pl.multiple_of(top + HALF, HALF), HALF), head_cols(step % H)

    def key_side(step):
        top, low, cols = bands(step)
        g0, g1, v0, v1 = g[top, cols], g[low, cols], v[top, cols], v[low, cols]
        s00 = jnp.where(causal, nt(g0, v0), 0.0).astype(BF16)
        s10 = nt(g1, v0).astype(BF16)
        s11 = jnp.where(causal, nt(g1, v1), 0.0).astype(BF16)
        scores[step, 0], scores[step, 1], scores[step, 2] = s00, s10, s11
        q0, q1 = q[top, cols], q[low, cols]
        ki[top, cols] = (tn(s00, q0) + tn(s10, q1)).astype(BF16)
        ki[low, cols] = tn(s11, q1).astype(BF16)

    def state_of(stream, h):
        return final[stream, pl.ds(2 * h, 2)].reshape(HD, HD)

    def key_end(step):
        top, low, cols = bands(step)
        h = step % H
        state = (state_of(QG, h).astype(F32) + jnp.where(step < H, qg1[h].astype(F32), 0.0)).astype(BF16)
        for band in (top, low):
            dk[band, cols] = ((ki[band, cols].astype(F32) + nn(v[band, cols], state)) * att_scale).astype(BF16)

    def query_end(step):
        top, low, cols = bands(step)
        h = step % H
        state = (state_of(KV, h).astype(F32) + jnp.where(step >= H, kv0[h], 0.0)).astype(BF16)
        k0, k1 = k[top, cols], k[low, cols]
        dq[top, cols] = ((nn(scores[step, 0], k0) + nt(g[top, cols], state)) * att_scale).astype(BF16)
        dq[low, cols] = (
            (nn(scores[step, 1], k0) + nn(scores[step, 2], k1) + nt(g[low, cols], state)) * att_scale
        ).astype(BF16)

    def before_scan(step):
        pair = (1 - core) * 2 + step % 2
        band = pl.ds(pl.multiple_of((step // 2) * 256, 256), 256)
        cols = pl.ds(pl.multiple_of(pair * 256, 256), 256)
        upper = nn(xt[band, 0:BLK], v[0:BLK, cols])
        lower = nn(xt[band, BLK : 2 * BLK], v[BLK : 2 * BLK, cols])
        xv[band, cols] = (upper + lower).astype(BF16)
        pre[band, cols] = nn(xt[band, :], ki[:, cols]) + nn(
            upper.astype(BF16), diagonal(qg1[2 * pair], qg1[2 * pair + 1])
        )

    def lay(made, m, color, keep):
        hi = m // 2
        for part in range(8):
            in_y, in_x = (m % 2) * 2 + part // 4, part % 4
            for lo in range(2):
                piece = made[part * 32 : part * 32 + 32, lo * 128 : lo * 128 + 128].astype(keep.dtype)
                if color == 0:
                    keep[color, in_x, in_y, hi, lo] = piece
                else:
                    keep[color, in_y, in_x, hi, lo] = piece

    def after_scan(color):
        pair = (1 - core) * 2 + color
        cols = pl.ds(pl.multiple_of(pair * 256, 256), 256)
        state = diagonal(state_of(QG, 2 * pair), state_of(QG, 2 * pair + 1))

        def body(m):
            band = pl.ds(pl.multiple_of(m * 256, 256), 256)
            lay((pre[band, cols] + nn(xv[band, cols], state)) * (att_scale * grad_scale), m, color, give)

        return body

    def product(color):
        cols = pl.ds(pl.multiple_of((core * 2 + color) * 256, 256), 256)

        def body(m):
            band = pl.ds(pl.multiple_of(m * 256, 256), 256)
            lay(nn(xt[band, :], dk[:, cols]) * grad_scale, m, color, mine)

        return body

    def key_pair(half, color):
        return lambda step: key_end((step // 2) * H + half * 4 + color * 2 + step % 2)

    loads[0].wait()
    loads[1].wait()
    states(QG, g, q, qg1, 1, (0, H // 2))
    loads[2].wait()
    loads[3].wait()
    load((k_hbm, k), (v_hbm, v), (x_hbm, x))
    states(QG, g, q, qg1, 1, (H // 2, H))
    pl.semaphore_wait(barrier, len(peers))
    spread(QG)
    loads[4].wait()
    loads[5].wait()
    states(KV, k, v, kv0, 0, (0, H))
    loads[6].wait()
    load((master_hbm, master), (m1_hbm, m1), (m2_hbm, m2))
    pl.loop(0, N1, unroll=2)(key_side)
    gather(QG)
    share(QG)
    spread(KV)
    pl.loop(N1, N2, unroll=2)(key_side)
    answer(QG)

    @pl.loop(0, 4)
    def _(m):
        band = pl.ds(pl.multiple_of(m * 256, 256), 256)
        xt[band, :] = x[:, band].T

    pl.loop(N2, 16, unroll=2)(key_side)
    gather(KV)
    share(KV)
    pl.loop(0, 8, unroll=2)(before_scan)
    answered(QG)

    for color in range(2):
        pl.loop(0, 4, unroll=2)(after_scan(color))
        sent.append(send(give.at[color], r0.at[color], s0.at[color], q0.at[color], partner))
    answer(KV)

    lines = ((at_x, along_x), (at_y, along_y))
    def ahead(color, n, to, rows, peer, relay=None):
        part = mine[color, to, rows] + r0[color, to, rows].astype(F32)
        if relay is not None:
            arrived(r1.at[color, relay], q1.at[color, relay])
            part = part + r1[color, relay].astype(F32)
        b[color, n] = part.astype(BF16)
        sent.append(send(b.at[color, n], r1.at[color, n], s1.at[color, n], q1.at[color, n], peer))

    first, second = slice(0, 2), slice(2, 4)
    for color in range(2):
        here, line = lines[color]
        pl.loop(0, 4, unroll=2)(key_pair(core, color))
        pl.loop(0, 4, unroll=2)(product(color))
        arrived(r0.at[color], q0.at[color])
        up, across, down = (here + 1) % 4, (here + 2) % 4, (here + 3) % 4
        ahead(color, 0, across, first, line[0])
        ahead(color, 1, across, second, line[2])
        ahead(color, 2, up, second, line[0])
        ahead(color, 4, down, first, line[2])
        mine[color, here] = mine[color, here] + r0[color, here].astype(F32)
    for color in range(2):
        here, line = lines[color]
        ahead(color, 3, (here + 1) % 4, first, line[0], 0)
        ahead(color, 5, (here + 3) % 4, second, line[2], 1)
        pl.loop(0, 4, unroll=2)(key_pair(1 - core, color))
    outs = []
    copy = pltpu.make_async_copy(dk, dk_hbm, out_sem.at[16])
    copy.start()
    outs.append(copy)
    answered(KV)
    pl.loop(0, M1, unroll=2)(query_end)
    for color in range(2):
        here = lines[color][0]
        there, line = lines[1 - color]
        for n in range(2, 6):
            arrived(r1.at[color, n], q1.at[color, n])
        mine[color, here, first] = mine[color, here, first] + r1[color, 3].astype(F32) + r1[color, 4].astype(F32)
        mine[color, here, second] = mine[color, here, second] + r1[color, 2].astype(F32) + r1[color, 5].astype(F32)
        for o in (2, 1, 3):
            to = (there + o) % 4
            c[color, o] = mine[color, here, to].astype(BF16)
            sent.append(send(c.at[color, o], r2.at[color, o], s2.at[color, o], q2.at[color, o], line[o - 1]))
    for color in range(2):
        here, there = lines[color][0], lines[1 - color][0]
        for o in range(1, 4):
            arrived(r2.at[color, o], q2.at[color, o])
        done[:, color] = (
            mine[color, here, there] + r2[color, 1].astype(F32) + r2[color, 2].astype(F32) + r2[color, 3].astype(F32)
        )
    w[...] = done[...].astype(BF16)
    for o in (2, 1, 3):
        to = (z + o) % 4
        peer = ((to % 2) * 2 + core, (to // 2) * PLANE + p)
        sent.append(send(w.at[to // 2], r3.at[o], s3.at[o], q3.at[o], peer))
    for o in range(1, 4):
        arrived(r3.at[o], q3.at[o])
    for copy in loads[7:]:
        copy.wait()
    summed[...] = done[z_hi] + r3[1].astype(F32) + r3[2].astype(F32) + r3[3].astype(F32)
    fresh = []
    for t in range(4):
        cols = pl.ds(pl.multiple_of(core * 512 + t * 128, 128), 128)
        grad = summed[t // 2, t % 2]
        grad_ref[:, cols] = grad
        fresh.append(adam(grad, master[:, cols], m1[:, cols], m2[:, cols])[0].astype(BF16))

    for color in range(2):
        here, there = lines[color][0], lines[1 - color][0]
        for lo in range(2):
            t = color * 2 + lo
            wide[color, here, z_hi, there, :, lo * 128 : lo * 128 + 128] = fresh[t]
    for color in range(2):
        here, there = lines[color][0], lines[1 - color][0]
        line = lines[1 - color][1]
        near = near_y if color == 0 else near_x
        spot = wide.at[color, here, z_hi, there]
        for o in (2, 1, 3):
            sent.append(send(spot, spot, s4.at[color, 1, o], q4.at[color, 1, o], near[o]))
            sent.append(send(spot, spot, s4.at[color, 0, o], q4.at[color, 0, o], line[o - 1]))
        sent.append(send(spot, spot, s4.at[color, 1, 0], q4.at[color, 1, 0], near[0]))
    sent.append(send(summed, other_sum, pair_sem.at[0], pair_sem.at[1], partner))
    def quarter(color, src, near, part):
        return wide.at[color, src, (z_hi + near) % 2, pl.ds(2 * part, 2)]

    def onward(color, src, near, part, way, hop):
        spot = quarter(color, src, near, part)
        n = near * 2 + part
        peer = lines[color][1][2 * way]
        sent.append(send(spot, spot, s5.at[color, hop, way, n], q5.at[color, hop, way, n], peer))

    def landed(color, src, near, part, way, hop):
        arrived(quarter(color, src, near, part), q5.at[color, hop, way, near * 2 + part])

    for near in range(2):
        for color in range(2):
            here, there = lines[color][0], lines[1 - color][0]
            for o in range(near == 0, 4):
                arrived(wide.at[color, here, (z_hi + near) % 2, (there + 4 - o) % 4], q4.at[color, near, o])
            for turn in range(2):
                for way in range(2):
                    onward(color, here, near, (way + turn) % 2, way, 0)
    for color in range(2):
        here = lines[color][0]
        sent.append(send(wide.at[color, here], far.at[color, here], s6.at[color, 0], q6.at[color, 0], partner))

    def put(src, half, color, at, n):
        cols = pl.ds(pl.multiple_of(half * 512 + color * 256, 256), 256)
        dst = w_hbm.at[:, :, at, :, cols] if color == 0 else w_hbm.at[:, at, :, :, cols]
        copy = pltpu.make_async_copy(src, dst, out_sem.at[n])
        copy.start()
        outs.append(copy)

    pl.loop(M1, M2, unroll=2)(query_end)
    for near in range(2):
        for color in range(2):
            here = lines[color][0]
            for way in range(2):
                src = (here + 3 - 2 * way) % 4
                landed(color, src, near, way, way, 0)
                onward(color, src, near, way, way, 1)
        if near == 0:
            pl.loop(M2, M3, unroll=2)(query_end)
    for color in range(2):
        put(wide.at[color, lines[color][0]], core, color, lines[color][0], color * 8)
    pl.loop(M3, 16, unroll=2)(query_end)
    copy = pltpu.make_async_copy(dq, dq_hbm, out_sem.at[17])
    copy.start()
    outs.append(copy)
    for o in (1, 3, 2):
        for color in range(2):
            here = lines[color][0]
            src = (here + 4 - o) % 4
            for near in range(2):
                if o == 2:
                    for way in range(2):
                        landed(color, src, near, way, way, 1)
                else:
                    way = o // 2
                    landed(color, src, near, 1 - way, way, 0)
            sent.append(send(wide.at[color, src], far.at[color, src], s6.at[color, o], q6.at[color, o], partner))
            put(wide.at[color, src], core, color, src, color * 8 + o)
    for o in (0, 1, 3, 2):
        for color in range(2):
            here = lines[color][0]
            src = (here + 4 - o) % 4
            arrived(far.at[color, src], q6.at[color, o])
            put(far.at[color, src], 1 - core, color, src, color * 8 + 4 + o)
    arrived(other_sum, pair_sem.at[1])
    for t in range(4):
        cols = pl.ds(pl.multiple_of((1 - core) * 512 + t * 128, 128), 128)
        grad_ref[:, cols] = other_sum[t // 2, t % 2]
    for copy in sent:
        copy.wait_send()
    shared(QG)
    shared(KV)
    for copy in outs:
        copy.wait()


def kernel_call(att_scale, grad_scale, inputs, q, k, v, g, master, m1, m2):
    width = inputs.shape[1]
    dma = pltpu.SemaphoreType.DMA
    tile = (32, 128)
    piece = (HD // 2, HD)
    wide = (2, 4, 2, 4, 32, 256)
    big = pltpu.VMEM(q.shape, BF16)
    full = jax.ShapeDtypeStruct(q.shape, BF16)
    return pl.pallas_call(
        lambda *refs: kernel(att_scale, grad_scale, *refs),
        out_shape=(full, full, jax.ShapeDtypeStruct((2, 4, 4, 32, width), BF16), jax.ShapeDtypeStruct(master.shape, F32)),
        in_specs=[HBM] * 8,
        out_specs=(ANY, ANY, ANY, VMEM),
        scratch_shapes=[
            pltpu.VMEM(master.shape, F32), pltpu.VMEM(master.shape, F32), pltpu.VMEM(master.shape, F32),
            big, big, big, big, big, big, big, big, big, big,
            pltpu.VMEM((width, width), F32),
            pltpu.VMEM((2 * H, 3, HALF, HALF), BF16),
            pltpu.VMEM((H, HD, HD), BF16),
            pltpu.VMEM((H, HD, HD), F32),
            pltpu.VMEM((2, PLANE) + piece, BF16),
            pltpu.VMEM((2, PLANE) + piece, BF16),
            pltpu.VMEM((2, PLANE) + piece, F32),
            pltpu.VMEM((2,) + piece, BF16),
            pltpu.VMEM((2, GROUP) + piece, BF16),
            pltpu.VMEM((2, PLANE) + piece, BF16),
            pltpu.VMEM((2, PLANE) + piece, BF16),
            pltpu.VMEM((2, 4, 4, 2, 2) + tile, BF16),
            pltpu.VMEM((2, 4, 4, 2, 2) + tile, F32),
            pltpu.VMEM((2, 4, 4, 2, 2) + tile, BF16),
            pltpu.VMEM((2, 6, 2, 2, 2) + tile, BF16),
            pltpu.VMEM((2, 6, 2, 2, 2) + tile, BF16),
            pltpu.VMEM((2, 4, 2, 2) + tile, BF16),
            pltpu.VMEM((2, 4, 2, 2) + tile, BF16),
            pltpu.VMEM((4, 2, 2) + tile, BF16),
            pltpu.VMEM((2, 2, 2) + tile, BF16),
            pltpu.VMEM((2, 2, 2) + tile, F32),
            pltpu.VMEM((2, 2) + tile, F32),
            pltpu.VMEM((2, 2) + tile, F32),
            pltpu.VMEM(wide, BF16),
            pltpu.VMEM(wide, BF16),
            dma((10,)), dma((18,)),
            dma((2, PLANE)), dma((2, PLANE)), dma((2, GROUP)), dma((2, GROUP)), dma((2, PLANE)), dma((2, PLANE)),
            dma((2,)), dma((2,)), dma((2, 6)), dma((2, 6)), dma((2, 4)), dma((2, 4)),
            dma((4,)), dma((4,)), dma((2, 2, 4)), dma((2, 2, 4)),
            dma((2, 2, 2, 4)), dma((2, 2, 2, 4)), dma((2, 4)), dma((2, 4)), dma((2,)),
        ],
        compiler_params=pltpu.CompilerParams(collective_id=0, has_side_effects=True, vmem_limit_bytes=VM << 20),
        name="backward",
    )(*[pltpu.with_memory_space_constraint(a, pltpu.HBM) for a in (inputs, q, k, v, g, master, m1, m2)])


def finish(dq_in, dk_in, w_in, grad, master, m1, m2, dq, dk, w, new_master, new_m1, new_m2, sem):
    copies = []
    for n, (src, dst) in enumerate(((dq_in, dq), (dk_in, dk), (w_in, w))):
        copy = pltpu.make_async_copy(src, dst, sem.at[n])
        copy.start()
        copies.append(copy)
    new_master[...], new_m1[...], new_m2[...] = adam(grad[...], master[...], m1[...], m2[...])
    for copy in copies:
        copy.wait()


def finish_call(dq, dk, w, grad, master, m1, m2):
    shape = lambda a: jax.ShapeDtypeStruct(a.shape, a.dtype)
    return pl.pallas_call(
        finish,
        out_shape=(shape(dq), shape(dk), shape(w), shape(master), shape(master), shape(master)),
        in_specs=[ANY] * 3 + [VMEM] * 4,
        out_specs=(ANY,) * 3 + (VMEM,) * 3,
        scratch_shapes=[pltpu.SemaphoreType.DMA((3,))],
        compiler_params=pltpu.CompilerParams(vmem_limit_bytes=4 << 20),
        name="finish",
    )(dq, dk, w, grad, master, m1, m2)


def local(inputs, queries, keys, values, out_grad, master, moment1, moment2):
    total_tokens = inputs.shape[0] * lax.axis_size("outer") * lax.axis_size("inner")
    att_scale = 1.0 / math.sqrt(HD * total_tokens)
    grad_scale = 1.0 / math.sqrt(total_tokens)
    query_grad, key_grad, weights, grad = kernel_call(
        att_scale, grad_scale, inputs, queries, keys, values, out_grad, master, moment1, moment2
    )
    query_grad, key_grad, weights, new_master, first, second = finish_call(
        query_grad, key_grad, weights, grad, master, moment1, moment2
    )
    return query_grad, key_grad, new_master, first, second, weights.reshape(inputs.shape[1], -1)


def solution(mesh):
    tokens, shard = P(("outer", "inner"), None), P("inner", None)
    return jax.shard_map(
        local,
        mesh=mesh,
        in_specs=(tokens,) * 5 + (shard,) * 3,
        out_specs=(tokens, tokens, shard, shard, shard, P()),
        check_vma=False,
    )
```

```python
import math

import jax
import jax.numpy as jnp
from jax import lax
from jax.experimental import pallas as pl
from jax.experimental.pallas import tpu as pltpu
from jax.sharding import PartitionSpec as P

H = 8
HD = 128
BLK = 512
HALF = BLK // 2
PLANE = 16
N1, M1, M2, M3, VM = 8, 4, 8, 12, 47
GROUP = 8
MESH = pl.DeviceIdType.MESH
F32 = jnp.float32
BF16 = jnp.bfloat16
ANY = pl.BlockSpec(memory_space=pl.ANY)
HBM = pl.BlockSpec(memory_space=pltpu.HBM)
VMEM = pl.BlockSpec(memory_space=pltpu.VMEM)


def nt(a, b):
    return lax.dot_general(a, b, (((1,), (1,)), ((), ())), preferred_element_type=F32)


def tn(a, b):
    return lax.dot_general(a, b, (((0,), (0,)), ((), ())), preferred_element_type=F32)


def nn(a, b):
    return lax.dot_general(a, b, (((1,), (0,)), ((), ())), preferred_element_type=F32)


def place():
    outer, inner = lax.axis_index("outer"), lax.axis_index("inner")
    return outer, inner, outer // 2, outer % 2, inner // PLANE, inner % PLANE


def greet(barrier, peers):
    for peer in peers:
        pl.semaphore_signal(barrier, inc=1, device_id=peer, device_id_type=MESH)


def send(src, dst, send_sem, recv_sem, peer):
    copy = pltpu.make_async_remote_copy(
        src_ref=src, dst_ref=dst, send_sem=send_sem, recv_sem=recv_sem, device_id=peer, device_id_type=MESH
    )
    copy.start()
    return copy


def arrived(ref, sem):
    pltpu.make_async_copy(ref, ref, sem).wait()


def adam(grad, master, m1, m2):
    first = 0.9 * m1 + 0.1 * grad
    second = 0.95 * m2 + 0.05 * grad * grad
    new = master - 0.01 * (first / (jnp.sqrt(second) + 1e-08) + 0.1 * master)
    return new, first, second


def diagonal(first, second):
    zero = jnp.zeros_like(first)
    return jnp.concatenate([jnp.concatenate([first, zero], 1), jnp.concatenate([zero, second], 1)], 0)


def kernel(
    att_scale, grad_scale,
    x_hbm, q_hbm, k_hbm, v_hbm, g_hbm, master_hbm, m1_hbm, m2_hbm,
    dq_hbm, dk_hbm, w_hbm, grad_ref,
    master, m1, m2, x, q, k, v, g, xt, ki, xv, dq, dk, pre, scores, qg1, kv0,
    own, got, local, total, totals, back, final,
    give, mine, r0, r1, b, r2, c, r3, w, done, summed, other_sum, wide, far,
    in_sem, out_sem, a1, e1, a2, e2, a3, e3,
    s0, q0, s1, q1, s2, q2, s3, q3, s4, q4, s5, q5, s6, q6, pair_sem,
):
    outer, inner, z_lo, core, z_hi, p = place()
    at_y, at_x = p // 4, p % 4
    z = z_hi * 2 + z_lo
    at = z_lo * 4 + core * 2 + z_hi
    plane = [(outer, z_hi * PLANE + (p + o) % PLANE) for o in range(1, PLANE)]
    ranked = []
    for o in range(1, GROUP):
        other = (at + o) % GROUP
        ranked.append((other // 2, (other % 2) * PLANE + p))
    partner = (z_lo * 2 + 1 - core, inner)
    along_x = [(outer, z_hi * PLANE + at_y * 4 + (at_x + o) % 4) for o in range(1, 4)]
    along_y = [(outer, z_hi * PLANE + ((at_y + o) % 4) * 4 + at_x) for o in range(1, 4)]
    beside = (z + 4 + 2 * z_lo - 1) % 4
    beside_outer, beside_inner = (beside % 2) * 2 + core, (beside // 2) * PLANE
    near_x = [(beside_outer, beside_inner + at_y * 4 + (at_x + o) % 4) for o in range(4)]
    near_y = [(beside_outer, beside_inner + ((at_y + o) % 4) * 4 + at_x) for o in range(4)]
    far_first = (10, 6, 9, 11, 5, 7, 13, 14, 15, 1, 2, 3, 8, 4, 12)
    peers = [plane[o - 1] for o in far_first] + near_x[1:] + near_y[1:] + ranked
    barrier = pltpu.get_barrier_semaphore()
    loads = []

    def load(*pairs):
        for src, dst in pairs:
            copy = pltpu.make_async_copy(src, dst, in_sem.at[len(loads)])
            copy.start()
            loads.append(copy)

    for side in range(2):
        cols = slice(side * H // 2 * HD, (side + 1) * H // 2 * HD)
        load((g_hbm.at[:, cols], g.at[:, cols]), (q_hbm.at[:, cols], q.at[:, cols]))
    greet(barrier, peers)
    sent = []
    QG, KV = 0, 1

    def head_cols(h):
        return pl.ds(pl.multiple_of(h * HD, HD), HD)

    def states(stream, left, right, keep, kept, heads):
        @pl.loop(*heads, unroll=4)
        def _(h):
            cols = head_cols(h)
            blocks = [tn(left[n * BLK : (n + 1) * BLK, cols], right[n * BLK : (n + 1) * BLK, cols]) for n in range(2)]
            keep[h] = blocks[kept].astype(keep.dtype)
            both = (blocks[0] + blocks[1]).astype(BF16)
            own[stream, 2 * h] = both[0 : HD // 2]
            own[stream, 2 * h + 1] = both[HD // 2 :]

    def spread(stream):
        for o in range(1, PLANE):
            to = (p + o) % PLANE
            sent.append(send(own.at[stream, to], got.at[stream, p], a1.at[stream, o], e1.at[stream, p], plane[o - 1]))
        got[stream, p] = own[stream, p]

    def gather(stream):
        for o in range(1, PLANE):
            src = (p + PLANE - o) % PLANE
            arrived(got.at[stream, src], e1.at[stream, src])
        run = jnp.zeros((HD // 2, HD), F32)
        for j in range(PLANE) if stream == KV else reversed(range(PLANE)):
            local[stream, j] = run
            run = run + got[stream, j].astype(F32)
        total[stream] = run.astype(BF16)

    def wanted(stream, here, there):
        return there < here if stream == KV else there > here

    def share(stream):
        for o in range(1, GROUP):
            other = (at + o) % GROUP

            @pl.when(wanted(stream, other, at))
            def _():
                send(total.at[stream], totals.at[stream, at], a2.at[stream, o], e2.at[stream, at], ranked[o - 1])

    def shared(stream):
        for o in range(1, GROUP):
            other = (at + o) % GROUP

            @pl.when(wanted(stream, other, at))
            def _():
                arrived(total.at[stream], a2.at[stream, o])

    def answer(stream):
        for j in range(GROUP):
            @pl.when(wanted(stream, at, j))
            def _():
                arrived(totals.at[stream, j], e2.at[stream, j])

            @pl.when(jnp.logical_not(wanted(stream, at, j)))
            def _():
                totals[stream, j] = jnp.zeros((HD // 2, HD), BF16)
        base = totals[stream, 0].astype(F32)
        for j in range(1, GROUP):
            base = base + totals[stream, j].astype(F32)
        for o in range(1, PLANE):
            to = (p + o) % PLANE
            back[stream, to] = (local[stream, to] + base).astype(BF16)
            sent.append(send(back.at[stream, to], final.at[stream, p], a3.at[stream, o], e3.at[stream, p], plane[o - 1]))
        final[stream, p] = (local[stream, p] + base).astype(BF16)

    def answered(stream):
        for o in range(1, PLANE):
            src = (p + PLANE - o) % PLANE
            arrived(final.at[stream, src], e3.at[stream, src])

    rows = lax.broadcasted_iota(jnp.int32, (HALF, HALF), 0)
    lanes = lax.broadcasted_iota(jnp.int32, (HALF, HALF), 1)
    causal = rows >= lanes

    def bands(step):
        top = pl.multiple_of((step // H) * BLK, BLK)
        return pl.ds(top, HALF), pl.ds(pl.multiple_of(top + HALF, HALF), HALF), head_cols(step % H)

    def key_side(step):
        top, low, cols = bands(step)
        g0, g1, v0, v1 = g[top, cols], g[low, cols], v[top, cols], v[low, cols]
        s00 = jnp.where(causal, nt(g0, v0), 0.0).astype(BF16)
        s10 = nt(g1, v0).astype(BF16)
        s11 = jnp.where(causal, nt(g1, v1), 0.0).astype(BF16)
        scores[step, 0], scores[step, 1], scores[step, 2] = s00, s10, s11
        q0, q1 = q[top, cols], q[low, cols]
        ki[top, cols] = (tn(s00, q0) + tn(s10, q1)).astype(BF16)
        ki[low, cols] = tn(s11, q1).astype(BF16)

    def state_of(stream, h):
        return final[stream, pl.ds(2 * h, 2)].reshape(HD, HD)

    def key_end(step):
        top, low, cols = bands(step)
        h = step % H
        state = (state_of(QG, h).astype(F32) + jnp.where(step < H, qg1[h].astype(F32), 0.0)).astype(BF16)
        for band in (top, low):
            dk[band, cols] = ((ki[band, cols].astype(F32) + nn(v[band, cols], state)) * att_scale).astype(BF16)

    def query_end(step):
        top, low, cols = bands(step)
        h = step % H
        state = (state_of(KV, h).astype(F32) + jnp.where(step >= H, kv0[h], 0.0)).astype(BF16)
        k0, k1 = k[top, cols], k[low, cols]
        dq[top, cols] = ((nn(scores[step, 0], k0) + nt(g[top, cols], state)) * att_scale).astype(BF16)
        dq[low, cols] = (
            (nn(scores[step, 1], k0) + nn(scores[step, 2], k1) + nt(g[low, cols], state)) * att_scale
        ).astype(BF16)

    def before_scan(step):
        pair = (1 - core) * 2 + step % 2
        band = pl.ds(pl.multiple_of((step // 2) * 256, 256), 256)
        cols = pl.ds(pl.multiple_of(pair * 256, 256), 256)
        upper = nn(xt[band, 0:BLK], v[0:BLK, cols])
        lower = nn(xt[band, BLK : 2 * BLK], v[BLK : 2 * BLK, cols])
        xv[band, cols] = (upper + lower).astype(BF16)
        pre[band, cols] = nn(xt[band, :], ki[:, cols]) + nn(
            upper.astype(BF16), diagonal(qg1[2 * pair], qg1[2 * pair + 1])
        )

    def lay(made, m, color, keep):
        hi = m // 2
        for part in range(8):
            in_y, in_x = (m % 2) * 2 + part // 4, part % 4
            for lo in range(2):
                piece = made[part * 32 : part * 32 + 32, lo * 128 : lo * 128 + 128].astype(keep.dtype)
                if color == 0:
                    keep[color, in_x, in_y, hi, lo] = piece
                else:
                    keep[color, in_y, in_x, hi, lo] = piece

    def after_scan(color):
        pair = (1 - core) * 2 + color
        cols = pl.ds(pl.multiple_of(pair * 256, 256), 256)
        state = diagonal(state_of(QG, 2 * pair), state_of(QG, 2 * pair + 1))

        def body(m):
            band = pl.ds(pl.multiple_of(m * 256, 256), 256)
            lay((pre[band, cols] + nn(xv[band, cols], state)) * (att_scale * grad_scale), m, color, give)

        return body

    def product(color):
        cols = pl.ds(pl.multiple_of((core * 2 + color) * 256, 256), 256)

        def body(m):
            band = pl.ds(pl.multiple_of(m * 256, 256), 256)
            lay(nn(xt[band, :], dk[:, cols]) * grad_scale, m, color, mine)

        return body

    def key_pair(half, color):
        return lambda step: key_end((step // 2) * H + half * 4 + color * 2 + step % 2)

    loads[0].wait()
    loads[1].wait()
    states(QG, g, q, qg1, 1, (0, H // 2))
    loads[2].wait()
    loads[3].wait()
    load((k_hbm, k), (v_hbm, v), (x_hbm, x))
    states(QG, g, q, qg1, 1, (H // 2, H))
    pl.semaphore_wait(barrier, len(peers))
    spread(QG)
    loads[4].wait()
    loads[5].wait()
    states(KV, k, v, kv0, 0, (0, H))
    loads[6].wait()
    load((master_hbm, master), (m1_hbm, m1), (m2_hbm, m2))
    pl.loop(0, N1, unroll=4)(key_side)
    gather(QG)
    share(QG)
    spread(KV)
    pl.loop(N1, 16, unroll=4)(key_side)
    answer(QG)

    @pl.loop(0, 4)
    def _(m):
        band = pl.ds(pl.multiple_of(m * 256, 256), 256)
        xt[band, :] = x[:, band].T

    pl.loop(0, 8, unroll=4)(before_scan)
    answered(QG)

    for color in range(2):
        pl.loop(0, 4, unroll=4)(after_scan(color))
        sent.append(send(give.at[color], r0.at[color], s0.at[color], q0.at[color], partner))
    lines = ((at_x, along_x), (at_y, along_y))
    def ahead(color, n, to, rows, peer, relay=None):
        part = mine[color, to, rows] + r0[color, to, rows].astype(F32)
        if relay is not None:
            arrived(r1.at[color, relay], q1.at[color, relay])
            part = part + r1[color, relay].astype(F32)
        b[color, n] = part.astype(BF16)
        sent.append(send(b.at[color, n], r1.at[color, n], s1.at[color, n], q1.at[color, n], peer))

    first, second = slice(0, 2), slice(2, 4)
    for color in range(2):
        here, line = lines[color]
        pl.loop(0, 4, unroll=4)(key_pair(core, color))
        pl.loop(0, 4, unroll=4)(product(color))
        arrived(r0.at[color], q0.at[color])
        up, across, down = (here + 1) % 4, (here + 2) % 4, (here + 3) % 4
        ahead(color, 0, across, first, line[0])
        ahead(color, 1, across, second, line[2])
        ahead(color, 2, up, second, line[0])
        ahead(color, 4, down, first, line[2])
        mine[color, here] = mine[color, here] + r0[color, here].astype(F32)
    gather(KV)
    share(KV)
    for color in range(2):
        here, line = lines[color]
        ahead(color, 3, (here + 1) % 4, first, line[0], 0)
        ahead(color, 5, (here + 3) % 4, second, line[2], 1)
        pl.loop(0, 4, unroll=4)(key_pair(1 - core, color))
    outs = []
    copy = pltpu.make_async_copy(dk, dk_hbm, out_sem.at[16])
    copy.start()
    outs.append(copy)
    for color in range(2):
        here = lines[color][0]
        there, line = lines[1 - color]
        for n in range(2, 6):
            arrived(r1.at[color, n], q1.at[color, n])
        mine[color, here, first] = mine[color, here, first] + r1[color, 3].astype(F32) + r1[color, 4].astype(F32)
        mine[color, here, second] = mine[color, here, second] + r1[color, 2].astype(F32) + r1[color, 5].astype(F32)
        for o in (2, 1, 3):
            to = (there + o) % 4
            c[color, o] = mine[color, here, to].astype(BF16)
            sent.append(send(c.at[color, o], r2.at[color, o], s2.at[color, o], q2.at[color, o], line[o - 1]))
    answer(KV)
    for color in range(2):
        here, there = lines[color][0], lines[1 - color][0]
        for o in range(1, 4):
            arrived(r2.at[color, o], q2.at[color, o])
        done[:, color] = (
            mine[color, here, there] + r2[color, 1].astype(F32) + r2[color, 2].astype(F32) + r2[color, 3].astype(F32)
        )
    w[...] = done[...].astype(BF16)
    for o in (2, 1, 3):
        to = (z + o) % 4
        peer = ((to % 2) * 2 + core, (to // 2) * PLANE + p)
        sent.append(send(w.at[to // 2], r3.at[o], s3.at[o], q3.at[o], peer))
    for o in range(1, 4):
        arrived(r3.at[o], q3.at[o])
    for copy in loads[7:]:
        copy.wait()
    summed[...] = done[z_hi] + r3[1].astype(F32) + r3[2].astype(F32) + r3[3].astype(F32)
    fresh = []
    for t in range(4):
        cols = pl.ds(pl.multiple_of(core * 512 + t * 128, 128), 128)
        grad = summed[t // 2, t % 2]
        grad_ref[:, cols] = grad
        fresh.append(adam(grad, master[:, cols], m1[:, cols], m2[:, cols])[0].astype(BF16))

    for color in range(2):
        here, there = lines[color][0], lines[1 - color][0]
        for lo in range(2):
            t = color * 2 + lo
            wide[color, here, z_hi, there, :, lo * 128 : lo * 128 + 128] = fresh[t]
    for color in range(2):
        here, there = lines[color][0], lines[1 - color][0]
        line = lines[1 - color][1]
        near = near_y if color == 0 else near_x
        spot = wide.at[color, here, z_hi, there]
        for o in (2, 1, 3):
            sent.append(send(spot, spot, s4.at[color, 1, o], q4.at[color, 1, o], near[o]))
            sent.append(send(spot, spot, s4.at[color, 0, o], q4.at[color, 0, o], line[o - 1]))
        sent.append(send(spot, spot, s4.at[color, 1, 0], q4.at[color, 1, 0], near[0]))
    sent.append(send(summed, other_sum, pair_sem.at[0], pair_sem.at[1], partner))
    answered(KV)
    pl.loop(0, M1, unroll=4)(query_end)
    def quarter(color, src, near, part):
        return wide.at[color, src, (z_hi + near) % 2, pl.ds(2 * part, 2)]

    def onward(color, src, near, part, way, hop):
        spot = quarter(color, src, near, part)
        n = near * 2 + part
        peer = lines[color][1][2 * way]
        sent.append(send(spot, spot, s5.at[color, hop, way, n], q5.at[color, hop, way, n], peer))

    def landed(color, src, near, part, way, hop):
        arrived(quarter(color, src, near, part), q5.at[color, hop, way, near * 2 + part])

    for near in range(2):
        for color in range(2):
            here, there = lines[color][0], lines[1 - color][0]
            for o in range(near == 0, 4):
                arrived(wide.at[color, here, (z_hi + near) % 2, (there + 4 - o) % 4], q4.at[color, near, o])
            for turn in range(2):
                for way in range(2):
                    onward(color, here, near, (way + turn) % 2, way, 0)
    for color in range(2):
        here = lines[color][0]
        sent.append(send(wide.at[color, here], far.at[color, here], s6.at[color, 0], q6.at[color, 0], partner))

    def put(src, half, color, at, n):
        cols = pl.ds(pl.multiple_of(half * 512 + color * 256, 256), 256)
        dst = w_hbm.at[:, :, at, :, cols] if color == 0 else w_hbm.at[:, at, :, :, cols]
        copy = pltpu.make_async_copy(src, dst, out_sem.at[n])
        copy.start()
        outs.append(copy)

    pl.loop(M1, M2, unroll=4)(query_end)
    for near in range(2):
        for color in range(2):
            here = lines[color][0]
            for way in range(2):
                src = (here + 3 - 2 * way) % 4
                landed(color, src, near, way, way, 0)
                onward(color, src, near, way, way, 1)
        if near == 0:
            pl.loop(M2, M3, unroll=4)(query_end)
    for color in range(2):
        put(wide.at[color, lines[color][0]], core, color, lines[color][0], color * 8)
    pl.loop(M3, 16, unroll=4)(query_end)
    copy = pltpu.make_async_copy(dq, dq_hbm, out_sem.at[17])
    copy.start()
    outs.append(copy)
    for o in (1, 3, 2):
        for color in range(2):
            here = lines[color][0]
            src = (here + 4 - o) % 4
            for near in range(2):
                if o == 2:
                    for way in range(2):
                        landed(color, src, near, way, way, 1)
                else:
                    way = o // 2
                    landed(color, src, near, 1 - way, way, 0)
            sent.append(send(wide.at[color, src], far.at[color, src], s6.at[color, o], q6.at[color, o], partner))
            put(wide.at[color, src], core, color, src, color * 8 + o)
    for o in (0, 1, 3, 2):
        for color in range(2):
            here = lines[color][0]
            src = (here + 4 - o) % 4
            arrived(far.at[color, src], q6.at[color, o])
            put(far.at[color, src], 1 - core, color, src, color * 8 + 4 + o)
    arrived(other_sum, pair_sem.at[1])
    for t in range(4):
        cols = pl.ds(pl.multiple_of((1 - core) * 512 + t * 128, 128), 128)
        grad_ref[:, cols] = other_sum[t // 2, t % 2]
    for copy in sent:
        copy.wait_send()
    shared(QG)
    shared(KV)
    for copy in outs:
        copy.wait()


def kernel_call(att_scale, grad_scale, inputs, q, k, v, g, master, m1, m2):
    width = inputs.shape[1]
    dma = pltpu.SemaphoreType.DMA
    tile = (32, 128)
    piece = (HD // 2, HD)
    wide = (2, 4, 2, 4, 32, 256)
    big = pltpu.VMEM(q.shape, BF16)
    full = jax.ShapeDtypeStruct(q.shape, BF16)
    return pl.pallas_call(
        lambda *refs: kernel(att_scale, grad_scale, *refs),
        out_shape=(full, full, jax.ShapeDtypeStruct((2, 4, 4, 32, width), BF16), jax.ShapeDtypeStruct(master.shape, F32)),
        in_specs=[HBM] * 8,
        out_specs=(ANY, ANY, ANY, VMEM),
        scratch_shapes=[
            pltpu.VMEM(master.shape, F32), pltpu.VMEM(master.shape, F32), pltpu.VMEM(master.shape, F32),
            big, big, big, big, big, big, big, big, big, big,
            pltpu.VMEM((width, width), F32),
            pltpu.VMEM((2 * H, 3, HALF, HALF), BF16),
            pltpu.VMEM((H, HD, HD), BF16),
            pltpu.VMEM((H, HD, HD), F32),
            pltpu.VMEM((2, PLANE) + piece, BF16),
            pltpu.VMEM((2, PLANE) + piece, BF16),
            pltpu.VMEM((2, PLANE) + piece, F32),
            pltpu.VMEM((2,) + piece, BF16),
            pltpu.VMEM((2, GROUP) + piece, BF16),
            pltpu.VMEM((2, PLANE) + piece, BF16),
            pltpu.VMEM((2, PLANE) + piece, BF16),
            pltpu.VMEM((2, 4, 4, 2, 2) + tile, BF16),
            pltpu.VMEM((2, 4, 4, 2, 2) + tile, F32),
            pltpu.VMEM((2, 4, 4, 2, 2) + tile, BF16),
            pltpu.VMEM((2, 6, 2, 2, 2) + tile, BF16),
            pltpu.VMEM((2, 6, 2, 2, 2) + tile, BF16),
            pltpu.VMEM((2, 4, 2, 2) + tile, BF16),
            pltpu.VMEM((2, 4, 2, 2) + tile, BF16),
            pltpu.VMEM((4, 2, 2) + tile, BF16),
            pltpu.VMEM((2, 2, 2) + tile, BF16),
            pltpu.VMEM((2, 2, 2) + tile, F32),
            pltpu.VMEM((2, 2) + tile, F32),
            pltpu.VMEM((2, 2) + tile, F32),
            pltpu.VMEM(wide, BF16),
            pltpu.VMEM(wide, BF16),
            dma((10,)), dma((18,)),
            dma((2, PLANE)), dma((2, PLANE)), dma((2, GROUP)), dma((2, GROUP)), dma((2, PLANE)), dma((2, PLANE)),
            dma((2,)), dma((2,)), dma((2, 6)), dma((2, 6)), dma((2, 4)), dma((2, 4)),
            dma((4,)), dma((4,)), dma((2, 2, 4)), dma((2, 2, 4)),
            dma((2, 2, 2, 4)), dma((2, 2, 2, 4)), dma((2, 4)), dma((2, 4)), dma((2,)),
        ],
        compiler_params=pltpu.CompilerParams(collective_id=0, has_side_effects=True, vmem_limit_bytes=VM << 20),
        name="backward",
    )(*[pltpu.with_memory_space_constraint(a, pltpu.HBM) for a in (inputs, q, k, v, g, master, m1, m2)])


def finish(dq_in, dk_in, w_in, grad, master, m1, m2, dq, dk, w, new_master, new_m1, new_m2, sem):
    copies = []
    for n, (src, dst) in enumerate(((dq_in, dq), (dk_in, dk), (w_in, w))):
        parts = src.shape[0] // 2
        for side in range(2):
            rows = slice(side * parts, (side + 1) * parts)
            copy = pltpu.make_async_copy(src.at[rows], dst.at[rows], sem.at[2 * n + side])
            copy.start()
            copies.append(copy)
    new_master[...], new_m1[...], new_m2[...] = adam(grad[...], master[...], m1[...], m2[...])
    for copy in copies:
        copy.wait()


def finish_call(dq, dk, w, grad, master, m1, m2):
    shape = lambda a: jax.ShapeDtypeStruct(a.shape, a.dtype)
    return pl.pallas_call(
        finish,
        out_shape=(shape(dq), shape(dk), shape(w), shape(master), shape(master), shape(master)),
        in_specs=[ANY] * 3 + [VMEM] * 4,
        out_specs=(ANY,) * 3 + (VMEM,) * 3,
        scratch_shapes=[pltpu.SemaphoreType.DMA((6,))],
        compiler_params=pltpu.CompilerParams(vmem_limit_bytes=4 << 20),
        name="finish",
    )(dq, dk, w, grad, master, m1, m2)


def local(inputs, queries, keys, values, out_grad, master, moment1, moment2):
    total_tokens = inputs.shape[0] * lax.axis_size("outer") * lax.axis_size("inner")
    att_scale = 1.0 / math.sqrt(HD * total_tokens)
    grad_scale = 1.0 / math.sqrt(total_tokens)
    query_grad, key_grad, weights, grad = kernel_call(
        att_scale, grad_scale, inputs, queries, keys, values, out_grad, master, moment1, moment2
    )
    query_grad, key_grad, weights, new_master, first, second = finish_call(
        query_grad, key_grad, weights, grad, master, moment1, moment2
    )
    return query_grad, key_grad, new_master, first, second, weights.reshape(inputs.shape[1], -1)


def solution(mesh):
    tokens, shard = P(("outer", "inner"), None), P("inner", None)
    return jax.shard_map(
        local,
        mesh=mesh,
        in_specs=(tokens,) * 5 + (shard,) * 3,
        out_specs=(tokens, tokens, shard, shard, shard, P()),
        check_vma=False,
    )
```
